32 devices in a mesh: scene: 4 (over y, x), expo: 8 (over z, core).
Axes of the slice: x: 2, y: 2, z: 4, core: 2. Of those that a mesh axis runs over, the one named last changes fastest.
Arguments:
- scene: bfloat16 [2048, 128, 128], P(('scene', 'expo')), may hold values from -6 to 6
- observed: bfloat16 [1024, 128, 128], P('expo'), may hold values from -9 to 9
- inverse_variance: bfloat16 [1024, 128, 128], P('expo'), may hold values from 0.25 to 4
- intersection: int32 [1024, 3], P('expo'), may hold values from 0 to 2047, as said below
- resample_index: int32 [1024, 6], P('expo'), may hold values from 0 to 31
- psf_index: int32 [1024], P('expo'), may hold values from 0 to 15
- resample_bank: bfloat16 [32, 128, 128], replicated, may hold values from -0.5 to 0.5
- psf_bank: bfloat16 [16, 128, 128], replicated, may hold values from -0.5 to 0.5
Outputs:
- gradient: float32 [2048, 128, 128], P(('scene', 'expo'))
The draws below stay inside these ranges and needn't reach their ends.
Inputs may be any that keep to these rules, and one draw needn't show every extreme that they name: `intersection`: the 3 scene blocks of exposure block j have 3 different owners and lie in sky strips j // 128 - 1 to j // 128 + 1; for each sky strip of exposure blocks, one owner appears in every one of its blocks.
All inputs are finite; a program needn't handle non-finite values.
Results may differ from the reference program's by a relative error of at most 0.014.
Values may be sent and summed in bfloat16 or wider, within the bound.
A program may use at most 128 MiB of HBM per device.

```python
import math
import jax
import jax.numpy as jnp
from jax import lax

P_SIZE = 128
K = 3
NW = 32
NPSF = 16
SB_DEV = 64
EB_DEV = 128
OWNERS = 4
STRIPS = 8
SB = 2048
EB = 1024


def draw_intersection(key, part):
    keys = jax.random.split(key, 6)
    blocks = jnp.arange(EB, dtype=jnp.int32)
    home = blocks // EB_DEV
    hot = jax.random.randint(keys[0], (STRIPS,), 0, OWNERS)[home]
    first = jax.random.randint(keys[1], (EB,), 1, OWNERS)
    second = jax.random.randint(keys[2], (EB,), 1, OWNERS - 1)
    second = jnp.where(second >= first, second + 1, second)
    owners_all = jnp.stack([hot, (hot + first) % OWNERS, (hot + second) % OWNERS], axis=1)
    turn = jax.random.randint(keys[3], (EB,), 0, K)
    order = (jnp.arange(K, dtype=jnp.int32)[None, :] + turn[:, None]) % K
    owners_all = jnp.take_along_axis(owners_all, order, axis=1)
    step_strip = jax.random.randint(keys[4], (EB, K), -1, 2)
    target = jnp.clip(home[:, None] + step_strip, 0, STRIPS - 1)
    within = jax.random.randint(keys[5], (EB, K), 0, SB_DEV)
    return (owners_all * (STRIPS * SB_DEV) + target * SB_DEV + within).astype(jnp.int32)


def plant(result, own_key, low, high):
    longest = result.shape.index(max(result.shape))
    spots = []
    for shift in (0, 1):
        where = [jax.random.randint(jax.random.fold_in(own_key, axis), (), 0, length) for axis, length in enumerate(result.shape)]
        where[longest] = (where[longest] + shift) % result.shape[longest]
        spots.append(tuple(where))
    return result.at[spots[0]].set(low).at[spots[1]].set(high)


def steps_of(stream_key, shape, shards, low, high):
    level = 1.0
    for dim, parts in shards:
        draws = jax.random.uniform(jax.random.fold_in(jax.random.fold_in(stream_key, 6), dim), (parts,), jnp.float32, low / len(shards), high / len(shards))
        level = level * jnp.repeat(jnp.exp(draws), shape[dim] // parts).reshape((-1,) + (1,) * (len(shape) - 1 - dim))
    return level


def gaussian(key, dims, deviation, reach, cuts=(), held_as=jnp.bfloat16):
    values = deviation * jax.random.normal(key, dims, jnp.float32)
    if cuts:
        values = values * steps_of(key, dims, cuts, -0.22, 0.18)
    return jnp.clip(values, -reach, reach).astype(held_as)


def setup_inputs(seed: int = 0) -> dict:
    seeds = jax.random.split(jax.random.key(seed), 9)
    return {
        "scene": gaussian(seeds[0], (SB, P_SIZE, P_SIZE), 1.0, 6.0, ((0, 32),)),
        "observed": gaussian(seeds[1], (EB, P_SIZE, P_SIZE), 1.5, 9.0, ((0, 8),)),
        "inverse_variance": jnp.clip(jnp.exp(math.log(4.0) - 2.7725887 * jax.random.uniform(seeds[2], (EB, P_SIZE, P_SIZE), jnp.float32) ** steps_of(seeds[2], (EB, P_SIZE, P_SIZE), ((0, 8),), -0.2, 0.2)), 0.25, 4.0).astype(jnp.bfloat16),
        "intersection": draw_intersection(jax.random.fold_in(seeds[8], 71), 0),
        "resample_index": plant(jax.random.randint(seeds[4], (EB, 2 * K), 0, NW), jax.random.fold_in(seeds[4], 1), 0, NW - 1).astype(jnp.int32),
        "psf_index": plant(jax.random.randint(seeds[5], (EB,), 0, NPSF), jax.random.fold_in(seeds[5], 1), 0, NPSF - 1).astype(jnp.int32),
        "resample_bank": gaussian(seeds[6], (NW, P_SIZE, P_SIZE), P_SIZE ** -0.5, 0.5),
        "psf_bank": gaussian(seeds[7], (NPSF, P_SIZE, P_SIZE), P_SIZE ** -0.5, 0.5),
    }


def reference(scene, observed, inverse_variance, intersection, resample_index, psf_index, resample_bank, psf_bank):
    total = jnp.zeros((EB, P_SIZE, P_SIZE), jnp.float32)
    for k in range(K):
        blocks = scene[intersection[:, k]].astype(jnp.float32)
        rows = resample_bank[resample_index[:, k]].astype(jnp.float32)
        cols = resample_bank[resample_index[:, K + k]].astype(jnp.float32)
        inner = jnp.einsum('jab,jcb->jac', blocks, cols).astype(jnp.bfloat16).astype(jnp.float32)
        term = jnp.einsum('jca,jab->jcb', rows, inner).astype(jnp.bfloat16)
        total = total + lax.optimization_barrier(term).astype(jnp.float32)
    resampled = total.astype(jnp.bfloat16).astype(jnp.float32)
    blur = psf_bank[psf_index].astype(jnp.float32)
    blurred_half = jnp.einsum('jab,jcb->jac', resampled, blur).astype(jnp.bfloat16).astype(jnp.float32)
    model = jnp.einsum('jca,jab->jcb', blur, blurred_half)
    weighted = (inverse_variance.astype(jnp.float32) * (model - observed.astype(jnp.float32))).astype(jnp.bfloat16).astype(jnp.float32)
    back_half = jnp.einsum('jab,jbc->jac', weighted, blur).astype(jnp.bfloat16).astype(jnp.float32)
    adjoint = jnp.einsum('jba,jbc->jac', blur, back_half).astype(jnp.bfloat16).astype(jnp.float32)
    gradient = jnp.zeros((SB, P_SIZE, P_SIZE), jnp.float32)
    for k in range(K):
        rows = resample_bank[resample_index[:, k]].astype(jnp.float32)
        cols = resample_bank[resample_index[:, K + k]].astype(jnp.float32)
        spread = jnp.einsum('jab,jbc->jac', adjoint, cols).astype(jnp.bfloat16).astype(jnp.float32)
        pulled = jnp.einsum('jba,jbc->jac', rows, spread)
        gradient = gradient.at[intersection[:, k]].add(pulled)
    return gradient
```

```python
import functools

import jax
import jax.numpy as jnp
from jax import lax
from jax.experimental import pallas as pl
from jax.experimental.pallas import tpu as pltpu
from jax.sharding import PartitionSpec as P

MESH = pl.DeviceIdType.MESH
UNROLL = 8
CHUNK = 8
VMEM_LIMIT = 56 * 1024 * 1024

READY, ROW, COL, PREV, PSF, LAST_LOW, LAST_HIGH, LAST_OWN = range(8)
GIVE, RANK = range(2)


def dot(a, b, dims):
    return lax.dot_general(a, b, (dims, ((), ())), preferred_element_type=jnp.float32)


NN = ((1,), (0,))
NT = ((1,), (1,))


class Plan:
    def __init__(self, owners, exposures):
        self.n = owners
        self.bits = owners.bit_length() - 1
        assert 1 << self.bits == owners
        self.exposures = exposures
        self.half = exposures // 2
        self.m = self.half // owners
        self.c = min(CHUNK, self.m)
        self.chunks = self.m // self.c

    def bit(self, h, p):
        return p if h == 0 else self.bits - 1 - p

    def value(self, owner, h, p):
        return (owner // (1 << self.bit(h, p))) % 2

    def partner(self, owner, h, p):
        step = 1 << self.bit(h, p)
        return owner + step - 2 * step * self.value(owner, h, p)

    def unit(self, owner, h, t):
        u = 0
        for p in range(self.bits):
            weight = self.n >> (p + 1)
            v = self.value(owner, h, p)
            u = u + weight * (v if t & weight else 1 - v)
        return h * self.half + u * self.m

    def base(self, h, t):
        return h * self.half + t * self.m

    def pull_turn(self, h, t, k):
        return (((self.n - 1 - t) * self.chunks + k) * 2 + h) * self.c

    def turns(self, owner, j):
        h, u, i = j // self.half, j % self.half // self.m, j % self.m
        me = [(self.unit(owner, h, self.n - 1) - h * self.half) // self.m for h in range(2)]
        apart = jnp.bitwise_xor(u, jnp.where(h == 0, me[0], me[1]))
        k, i = i // self.c, i % self.c
        first = (((self.n - 1 - apart) * self.chunks + k) * 2 + h) * self.c + i
        last = ((apart * self.chunks + k) * 2 + h) * self.c + i
        return first, last

    def phase(self, t):
        p = 0
        while t >= self.n - (self.n >> (p + 1)):
            p += 1
        return p


def fill_tables(plan, per_dev, kernels, owner, strip, strips, inter, index, psf_index, table, tell):
    e, width = plan.exposures, inter.shape[0]
    where = inter[...]
    match = where // (strips * per_dev) == owner
    place = (where // per_dev % strips - strip + 1) * per_dev + where % per_dev

    def pick(values):
        return jnp.sum(jnp.where(match, values, 0), axis=0, keepdims=True)

    live = pick(jnp.ones_like(where)) > 0
    slot = jnp.where(live, jnp.clip(pick(place), 0, 3 * per_dev - 1), -1)
    kernel_of = index[...]
    table[pl.ds(ROW, 1), :] = jnp.where(live, pick(kernel_of[:width]), kernels)
    table[pl.ds(COL, 1), :] = pick(kernel_of[width:])
    table[pl.ds(PSF, 1), :] = psf_index[...]

    down = lax.broadcasted_iota(jnp.int32, (e, e), 0)
    along = lax.broadcasted_iota(jnp.int32, (e, e), 1)
    first_along, last_along = plan.turns(owner, along)
    first_down, last_down = plan.turns(owner, down)
    del first_down

    def upright(line):
        return jnp.sum(jnp.where(down == along, line, 0), axis=1, keepdims=True)

    def flat(column):
        return jnp.sum(jnp.where(down == along, column, 0), axis=0, keepdims=True)

    slot_down = upright(slot)
    before = (slot_down == slot) & (last_down < last_along)
    table[pl.ds(PREV, 1), :] = jnp.max(jnp.where(before, last_down + 1, 0), axis=0, keepdims=True)

    ready = jnp.where(live, slot, per_dev)
    for side, last_row in ((0, LAST_LOW), (1, LAST_OWN), (2, LAST_HIGH)):
        near = slot - side * per_dev
        near = jnp.where((near >= 0) & (near < per_dev) & live, near, -1)
        hit = near == down
        last = jnp.max(jnp.where(hit, last_along + 1, 0), axis=1, keepdims=True)
        if side == 1:
            table[pl.ds(last_row, 1), :] = flat(last)
            continue
        line = down[:, :1]
        first = jnp.min(jnp.where(hit, first_along, e + down), axis=1, keepdims=True)
        rank = jnp.sum(jnp.where(flat(first) < first, 1, 0), axis=1, keepdims=True)
        give = jnp.sum(jnp.where(rank == along, down, 0), axis=0, keepdims=True)
        arrival = jnp.sum(jnp.where(hit, rank, 0), axis=0, keepdims=True)
        ready = jnp.where(near >= 0, side * per_dev + arrival, ready)
        order = jnp.where(line < per_dev, last, e + 1) * e + line
        order_along = flat(order)
        done = jnp.sum(jnp.where(order_along < order, 1, 0), axis=1, keepdims=True)
        table[pl.ds(last_row, 1), :] = jnp.sum(jnp.where(done == along, last, 0), axis=0, keepdims=True)
        up = side // 2
        tell[up, pl.ds(GIVE, 1), :] = jnp.clip(give, 0, per_dev - 1)
        tell[up, pl.ds(RANK, 1), :] = jnp.clip(flat(done), 0, per_dev - 1)
    table[pl.ds(READY, 1), :] = ready


def gradient_kernel(
    plan, per_dev, inter, index, psf_index, scene, observed, weights, bank_h, psf_h, out_h,
    table_v, tell_v, told_v, table, told, ready, stage, came, bank, bank_t, psf, psf_t, obs, ivar, terms, got,
    adj, run, leave, back, out, load_sem, tell_send, tell_recv, z_send, z_recv, rs_send, rs_recv, ag_send,
    ag_recv, back_send, back_recv, store_sem,
):
    n, m, c = plan.n, plan.m, plan.c
    e = plan.exposures
    kernels = bank_h.shape[0]
    owner = lax.axis_index("scene")
    strip = lax.axis_index("expo")
    strips = lax.axis_size("expo")
    pieces = per_dev // c
    has = {0: strip > 0, 1: strip < strips - 1}

    barrier = pltpu.get_barrier_semaphore()
    for p in range(plan.bits):
        pl.semaphore_signal(
            barrier, inc=1, device_id={"scene": plan.partner(owner, 0, p)}, device_id_type=MESH
        )
    for up in range(2):

        @pl.when(has[up])
        def _(up=up):
            pl.semaphore_signal(
                barrier, inc=1, device_id={"expo": strip + 2 * up - 1}, device_id_type=MESH
            )

    loads = [
        pltpu.make_async_copy(scene, ready.at[pl.ds(per_dev, per_dev)], load_sem.at[0]),
        pltpu.make_async_copy(bank_h, bank.at[pl.ds(0, kernels)], load_sem.at[1]),
        pltpu.make_async_copy(psf_h, psf, load_sem.at[2]),
    ]
    for h in range(2):
        home = plan.unit(owner, h, n - 1)
        for source, target in ((observed, obs), (weights, ivar)):
            loads.append(
                pltpu.make_async_copy(
                    source.at[pl.ds(home, m)], target.at[pl.ds(h * m, m)], load_sem.at[len(loads)]
                )
            )
    for load in loads:
        load.start()

    fill_tables(
        plan, per_dev, kernels, owner, strip, strips, inter, index, psf_index, table_v, tell_v
    )
    own_table = pltpu.make_async_copy(table_v, table, load_sem.at[7])
    own_table.start()
    pl.semaphore_wait(
        barrier, plan.bits + jnp.where(has[0], 1, 0) + jnp.where(has[1], 1, 0)
    )

    def tell_copy(up):
        return pltpu.make_async_remote_copy(
            src_ref=tell_v.at[up],
            dst_ref=told_v.at[1 - up],
            send_sem=tell_send.at[up],
            recv_sem=tell_recv.at[1 - up],
            device_id={"expo": strip + 2 * up - 1},
            device_id_type=MESH,
        )

    for up in range(2):

        @pl.when(has[up])
        def _(up=up):
            tell_copy(up).start()

    bank[kernels] = jnp.zeros(bank.shape[1:], bank.dtype)
    bank_t[kernels] = jnp.zeros(bank.shape[1:], bank.dtype)
    run[0] = jnp.zeros(run.shape[1:], run.dtype)
    loads[0].wait()
    for up in range(2):

        @pl.when(jnp.logical_not(has[up]))
        def _(up=up):
            told_v[up] = jnp.zeros(told_v.shape[1:], told_v.dtype)

            def wipe(i, carry):
                back[up * per_dev + i] = jnp.zeros(back.shape[1:], back.dtype)
                return carry

            lax.fori_loop(0, per_dev, wipe, 0)

        @pl.when(has[up])
        def _(up=up):
            tell_copy(1 - up).wait_recv()

    told_copy = pltpu.make_async_copy(told_v, told, load_sem.at[8])
    told_copy.start()
    told_copy.wait()

    def z_copy(up, q):
        where = up * per_dev + q * c
        return pltpu.make_async_remote_copy(
            src_ref=stage.at[pl.ds(where, c)],
            dst_ref=came.at[pl.ds(where, c)],
            send_sem=z_send.at[where // c],
            recv_sem=z_recv.at[where // c],
            device_id={"expo": strip + 2 * up - 1},
            device_id_type=MESH,
        )

    for q in range(pieces):
        for up in range(2):

            @pl.when(has[up])
            def _(up=up, q=q):
                def fill(i, carry):
                    stage[up * per_dev + q * c + i] = ready[per_dev + told[up, GIVE, q * c + i]]
                    return carry

                lax.fori_loop(0, c, fill, 0, unroll=2)
                z_copy(up, q).start()

    for load in loads[1:]:
        load.wait()

    def turn_bank(i, carry):
        bank_t[i] = bank[i].T
        return carry

    def turn_psf(i, carry):
        psf_t[i] = psf[i].T
        return carry

    lax.fori_loop(0, kernels, turn_bank, 0)
    lax.fori_loop(0, psf.shape[0], turn_psf, 0)
    own_table.wait()

    def take(q):
        for up in range(2):

            @pl.when(has[1 - up])
            def _(up=up):
                z_copy(up, q).wait_recv()

                def keep(i, carry):
                    a = q * c + i
                    ready[(1 - up) * 2 * per_dev + a] = came[up * per_dev + a]
                    return carry

                lax.fori_loop(0, c, keep, 0, unroll=2)

    def scatter_copy(h, t, k):
        where = plan.base(h, t) + k * c
        slot = where // c
        return pltpu.make_async_remote_copy(
            src_ref=terms.at[pl.ds(where, c)],
            dst_ref=got.at[pl.ds(where, c)],
            send_sem=rs_send.at[slot],
            recv_sem=rs_recv.at[slot],
            device_id={"scene": plan.partner(owner, h, plan.phase(t))},
            device_id_type=MESH,
        )

    def gather_copy(h, t, p, k):
        source = plan.base(h, t) + k * c
        target = plan.base(h, t - (n >> (p + 1))) + k * c
        slot = target // c
        return pltpu.make_async_remote_copy(
            src_ref=adj.at[pl.ds(source, c)],
            dst_ref=adj.at[pl.ds(target, c)],
            send_sem=ag_send.at[slot],
            recv_sem=ag_recv.at[slot],
            device_id={"scene": plan.partner(owner, h, p)},
            device_id_type=MESH,
        )

    def make_terms(h, t, k):
        where = plan.base(h, t) + k * c
        first = plan.unit(owner, h, t) + k * c

        def body(i, carry):
            at = [i * unroll + a for a in range(unroll)]
            inner = [
                dot(ready[table[READY, first + a]], bank_t[table[COL, first + a]], NN).astype(jnp.bfloat16)
                for a in at
            ]
            term = [dot(bank[table[ROW, first + a]], x, NN).astype(jnp.bfloat16) for a, x in zip(at, inner)]
            for a, x in zip(at, term):
                terms[where + a] = x
            return carry

        lax.fori_loop(0, c // unroll, body, 0)

    unroll = min(UNROLL, c)

    def arrived(t):
        return [t - (n >> (q + 1)) for q in range(plan.bits) if t >= n - (n >> (q + 1))]

    def summed(h, t, k, i):
        total = terms[plan.base(h, t) + k * c + i].astype(jnp.float32)
        for source in arrived(t):
            total = total + got[plan.base(h, source) + k * c + i].astype(jnp.float32)
        return total.astype(jnp.bfloat16)

    def pass_on(h, t, k):
        where = plan.base(h, t) + k * c

        def body(i, carry):
            terms[where + i] = summed(h, t, k, i)
            return carry

        lax.fori_loop(0, c, body, 0)

    def psf_pass(h, k):
        where = plan.base(h, n - 1) + k * c
        first = plan.unit(owner, h, n - 1) + k * c
        here = h * m + k * c

        def body(i, carry):
            at = [i * unroll + a for a in range(unroll)]
            which = [table[PSF, first + a] for a in at]
            half = [
                dot(summed(h, n - 1, k, a), psf_t[q], NN).astype(jnp.bfloat16) for a, q in zip(at, which)
            ]
            model = [dot(psf[q], x, NN) for q, x in zip(which, half)]
            weighted = [
                (ivar[here + a].astype(jnp.float32) * (x - obs[here + a].astype(jnp.float32))).astype(jnp.bfloat16)
                for a, x in zip(at, model)
            ]
            half = [dot(x, psf[q], NN).astype(jnp.bfloat16) for q, x in zip(which, weighted)]
            for a, q, x in zip(at, which, half):
                adj[where + a] = dot(psf_t[q], x, NN).astype(jnp.bfloat16)
            return carry

        lax.fori_loop(0, c // unroll, body, 0)

    for t in range(n):
        for k in range(plan.chunks):
            for h in range(2):
                q = (t * plan.chunks + k) * 2 + h
                if q < pieces:
                    take(q)
                make_terms(h, t, k)
                for source in arrived(t):
                    scatter_copy(h, source, k).wait_recv()
                if t < n // 2:
                    scatter_copy(h, t, k).start()
                elif t < n - 1:
                    pass_on(h, t, k)
                    scatter_copy(h, t, k).start()
                else:
                    psf_pass(h, k)
                    for p in reversed(range(plan.bits)):
                        gather_copy(h, n - 1, p, k).start()

    for up in range(2):

        @pl.when(has[up])
        def _(up=up):
            tell_copy(up).wait_send()
            for q in range(pieces):
                z_copy(up, q).wait_send()

    def back_copy(up, q):
        where = up * per_dev + q * c
        return pltpu.make_async_remote_copy(
            src_ref=leave.at[pl.ds(where, c)],
            dst_ref=back.at[pl.ds((1 - up) * per_dev + q * c, c)],
            send_sem=back_send.at[where // c],
            recv_sem=back_recv.at[((1 - up) * per_dev + q * c) // c],
            device_id={"expo": strip + 2 * up - 1},
            device_id_type=MESH,
        )

    def pull(h, t, k):
        where = plan.base(h, t) + k * c
        first = plan.unit(owner, h, t) + k * c
        turn = plan.pull_turn(h, t, k)

        def body(i, carry):
            at = [i * unroll + a for a in range(unroll)]
            spread = [
                dot(adj[where + a], bank[table[COL, first + a]], NN).astype(jnp.bfloat16) for a in at
            ]
            pulled = [dot(bank_t[table[ROW, first + a]], x, NN) for a, x in zip(at, spread)]
            for a, x in zip(at, pulled):
                run[1 + turn + a] = x + run[table[PREV, first + a]]
            return carry

        lax.fori_loop(0, c // unroll, body, 0)

        for q in range(pieces):
            due = max(c, e - per_dev + (q + 1) * c)
            if turn < due <= turn + c:
                for up, last in ((0, LAST_LOW), (1, LAST_HIGH)):

                    @pl.when(has[up])
                    def _(up=up, last=last, q=q):
                        def put(i, carry):
                            a = q * c + i
                            leave[up * per_dev + a] = run[table[last, a]].astype(leave.dtype)
                            return carry

                        lax.fori_loop(0, c, put, 0, unroll=2)
                        back_copy(up, q).start()

    for k in range(plan.chunks):
        for h in range(2):
            pull(h, n - 1, k)
    for last in reversed(range(plan.bits)):
        for t in reversed(range(n - (n >> last), n - (n >> (last + 1)))):
            for k in range(plan.chunks):
                for h in range(2):
                    gather_copy(h, t + (n >> (last + 1)), last, k).wait_recv()
                    for p in reversed(range(last)):
                        gather_copy(h, t, p, k).start()
                    pull(h, t, k)

    for t in range(n - 1):
        for k in range(plan.chunks):
            for h in range(2):
                scatter_copy(h, t, k).wait_send()
                p = plan.phase(t)
                gather_copy(h, t + (n >> (p + 1)), p, k).wait_send()

    for up in range(2):

        @pl.when(has[up])
        def _(up=up):
            for q in range(pieces):
                back_copy(1 - up, q).wait_recv()

    stores = []
    for q in range(pieces):

        def own(i, carry, q=q):
            b = q * c + i
            low = back[told[0, RANK, b]].astype(jnp.float32)
            high = back[per_dev + told[1, RANK, b]].astype(jnp.float32)
            out[b] = run[table[LAST_OWN, b]] + (low + high)
            return carry

        lax.fori_loop(0, c, own, 0, unroll=2)
        store = pltpu.make_async_copy(out.at[pl.ds(q * c, c)], out_h.at[pl.ds(q * c, c)], store_sem.at[q])
        store.start()
        stores.append(store)

    for up in range(2):

        @pl.when(has[up])
        def _(up=up):
            for q in range(pieces):
                back_copy(up, q).wait_send()

    for store in stores:
        store.wait()


def on_device(
    scene,
    observed,
    inverse_variance,
    intersection,
    resample_index,
    psf_index,
    resample_bank,
    psf_bank,
):
    per_dev, side = scene.shape[0], scene.shape[1:]
    e = intersection.shape[0]
    plan = Plan(lax.axis_size("scene"), e)
    slots = e // plan.c
    pieces = per_dev // plan.c
    kernels, psfs = resample_bank.shape[0], psf_bank.shape[0]
    dtype = scene.dtype
    vmem = pl.BlockSpec(memory_space=pltpu.VMEM)
    hbm = pl.BlockSpec(memory_space=pl.ANY)
    dma = pltpu.SemaphoreType.DMA
    blocks = lambda count, kind=dtype: pltpu.VMEM((count, *side), kind)
    return pl.pallas_call(
        functools.partial(gradient_kernel, plan, per_dev),
        out_shape=jax.ShapeDtypeStruct((per_dev, *side), jnp.float32),
        in_specs=[vmem] * 3 + [hbm] * 5,
        out_specs=hbm,
        scratch_shapes=[
            pltpu.VMEM((8, e), jnp.int32),
            pltpu.VMEM((2, 2, e), jnp.int32),
            pltpu.VMEM((2, 2, e), jnp.int32),
            pltpu.SMEM((8, e), jnp.int32),
            pltpu.SMEM((2, 2, e), jnp.int32),
            blocks(3 * per_dev),
            blocks(2 * per_dev),
            blocks(2 * per_dev),
            blocks(kernels + 1),
            blocks(kernels + 1),
            blocks(psfs),
            blocks(psfs),
            blocks(2 * plan.m),
            blocks(2 * plan.m),
            blocks(e),
            blocks(e),
            blocks(e),
            blocks(e + 1, jnp.float32),
            blocks(2 * per_dev),
            blocks(2 * per_dev),
            blocks(per_dev, jnp.float32),
            dma((9,)),
            dma((2,)),
            dma((2,)),
            dma((2 * pieces,)),
            dma((2 * pieces,)),
            dma((slots,)),
            dma((slots,)),
            dma((slots,)),
            dma((slots,)),
            dma((2 * pieces,)),
            dma((2 * pieces,)),
            dma((pieces,)),
        ],
        compiler_params=pltpu.CompilerParams(
            collective_id=0, has_side_effects=True, vmem_limit_bytes=VMEM_LIMIT
        ),
        name="gradient",
    )(
        intersection.T, resample_index.T, psf_index.reshape(1, e), scene, observed, inverse_variance,
        resample_bank, psf_bank,
    )


def solution(mesh):
    return jax.shard_map(
        on_device,
        mesh=mesh,
        in_specs=(
            P(("scene", "expo"), None, None),
            P("expo", None, None),
            P("expo", None, None),
            P("expo", None),
            P("expo", None),
            P("expo"),
            P(),
            P(),
        ),
        out_specs=P(("scene", "expo"), None, None),
        check_vma=False,
    )
```

```python
import functools

import jax
import jax.numpy as jnp
from jax import lax
from jax.experimental import pallas as pl
from jax.experimental.pallas import tpu as pltpu
from jax.sharding import PartitionSpec as P

MESH = pl.DeviceIdType.MESH
UNROLL = 4
CHUNK = 4
VMEM_LIMIT = 56 * 1024 * 1024

READY, ROW, COL, PREV, PSF, LAST_LOW, LAST_HIGH, LAST_OWN = range(8)
GIVE, RANK = range(2)


def dot(a, b, dims):
    return lax.dot_general(a, b, (dims, ((), ())), preferred_element_type=jnp.float32)


NN = ((1,), (0,))
NT = ((1,), (1,))


class Plan:
    def __init__(self, owners, exposures):
        self.n = owners
        self.bits = owners.bit_length() - 1
        assert 1 << self.bits == owners
        self.exposures = exposures
        self.half = exposures // 2
        self.m = self.half // owners
        self.c = min(CHUNK, self.m)
        self.chunks = self.m // self.c

    def bit(self, h, p):
        return p if h == 0 else self.bits - 1 - p

    def value(self, owner, h, p):
        return (owner // (1 << self.bit(h, p))) % 2

    def partner(self, owner, h, p):
        step = 1 << self.bit(h, p)
        return owner + step - 2 * step * self.value(owner, h, p)

    def unit(self, owner, h, t):
        u = 0
        for p in range(self.bits):
            weight = self.n >> (p + 1)
            v = self.value(owner, h, p)
            u = u + weight * (v if t & weight else 1 - v)
        return h * self.half + u * self.m

    def base(self, h, t):
        return h * self.half + t * self.m

    def hops(self, t):
        return 0 if t == self.n - 1 else 1 + self.hops(t + (self.n >> (self.phase(t) + 1)))

    def pulls(self):
        order, start = [], 0
        for hops in range(self.bits + 1):
            units = [t for t in reversed(range(self.n)) if self.hops(t) == hops]
            order.append((units, start))
            start += len(units) * self.chunks
        return order

    def turns(self, owner, j):
        h, u, i = j // self.half, j % self.half // self.m, j % self.m
        me = [(self.unit(owner, h, self.n - 1) - h * self.half) // self.m for h in range(2)]
        apart = jnp.bitwise_xor(u, jnp.where(h == 0, me[0], me[1]))
        k, i = i // self.c, i % self.c
        first = (((self.n - 1 - apart) * self.chunks + k) * 2 + h) * self.c + i
        place = jnp.zeros_like(j)
        for units, start in self.pulls():
            for at, t in enumerate(units):
                place = jnp.where(apart == self.n - 1 - t, start + k * len(units) + at, place)
        last = (place * 2 + h) * self.c + i
        return first, last

    def phase(self, t):
        p = 0
        while t >= self.n - (self.n >> (p + 1)):
            p += 1
        return p


def fill_tables(plan, per_dev, kernels, owner, strip, strips, inter, index, psf_index, table, tell):
    e, width = plan.exposures, inter.shape[0]
    where = inter[...]
    match = where // (strips * per_dev) == owner
    place = (where // per_dev % strips - strip + 1) * per_dev + where % per_dev

    def pick(values):
        return jnp.sum(jnp.where(match, values, 0), axis=0, keepdims=True)

    live = pick(jnp.ones_like(where)) > 0
    slot = jnp.where(live, jnp.clip(pick(place), 0, 3 * per_dev - 1), -1)
    kernel_of = index[...]
    table[pl.ds(ROW, 1), :] = jnp.where(live, pick(kernel_of[:width]), kernels)
    table[pl.ds(COL, 1), :] = pick(kernel_of[width:])
    table[pl.ds(PSF, 1), :] = psf_index[...]

    down = lax.broadcasted_iota(jnp.int32, (e, e), 0)
    along = lax.broadcasted_iota(jnp.int32, (e, e), 1)
    first_along, last_along = plan.turns(owner, along[:1])

    def upright(line):
        return jnp.sum(jnp.where(down == along, line, 0), axis=1, keepdims=True)

    def flat(column):
        return jnp.sum(jnp.where(down == along, column, 0), axis=0, keepdims=True)

    slot_down, last_down = upright(slot), upright(last_along)
    before = (slot_down == slot) & (last_down < last_along)
    table[pl.ds(PREV, 1), :] = jnp.max(jnp.where(before, last_down + 1, 0), axis=0, keepdims=True)

    ready = jnp.where(live, slot, per_dev)
    for side, last_row in ((0, LAST_LOW), (1, LAST_OWN), (2, LAST_HIGH)):
        near = slot - side * per_dev
        near = jnp.where((near >= 0) & (near < per_dev) & live, near, -1)
        hit = near == down
        last = jnp.max(jnp.where(hit, last_along + 1, 0), axis=1, keepdims=True)
        if side == 1:
            table[pl.ds(last_row, 1), :] = flat(last)
            continue
        line = down[:, :1]
        first = jnp.min(jnp.where(hit, first_along, e + down), axis=1, keepdims=True)
        rank = jnp.sum(jnp.where(flat(first) < first, 1, 0), axis=1, keepdims=True)
        give = jnp.sum(jnp.where(rank == along, down, 0), axis=0, keepdims=True)
        arrival = jnp.sum(jnp.where(hit, rank, 0), axis=0, keepdims=True)
        ready = jnp.where(near >= 0, side * per_dev + arrival, ready)
        order = jnp.where(line < per_dev, last, e + 1) * e + line
        order_along = flat(order)
        done = jnp.sum(jnp.where(order_along < order, 1, 0), axis=1, keepdims=True)
        table[pl.ds(last_row, 1), :] = jnp.sum(jnp.where(done == along, last, 0), axis=0, keepdims=True)
        up = side // 2
        tell[up, pl.ds(GIVE, 1), :] = jnp.clip(give, 0, per_dev - 1)
        tell[up, pl.ds(RANK, 1), :] = jnp.clip(flat(done), 0, per_dev - 1)
    table[pl.ds(READY, 1), :] = ready


def gradient_kernel(
    plan, per_dev, inter, index, psf_index, scene, observed, weights, bank_h, psf_h, out_h,
    table_v, tell_v, told_v, table, told, ready, stage, came, bank, bank_t, psf, psf_t, obs, ivar, terms, got,
    adj, run, leave, back, out, load_sem, tell_send, tell_recv, z_send, z_recv, rs_send, rs_recv, ag_send,
    ag_recv, back_send, back_recv, store_sem,
):
    n, m, c = plan.n, plan.m, plan.c
    e = plan.exposures
    kernels = bank_h.shape[0]
    owner = lax.axis_index("scene")
    strip = lax.axis_index("expo")
    strips = lax.axis_size("expo")
    pieces = per_dev // c
    has = {0: strip > 0, 1: strip < strips - 1}

    barrier = pltpu.get_barrier_semaphore()
    for p in range(plan.bits):
        pl.semaphore_signal(
            barrier, inc=1, device_id={"scene": plan.partner(owner, 0, p)}, device_id_type=MESH
        )
    for up in range(2):

        @pl.when(has[up])
        def _(up=up):
            pl.semaphore_signal(
                barrier, inc=1, device_id={"expo": strip + 2 * up - 1}, device_id_type=MESH
            )

    loads = [
        pltpu.make_async_copy(scene, ready.at[pl.ds(per_dev, per_dev)], load_sem.at[0]),
        pltpu.make_async_copy(bank_h, bank.at[pl.ds(0, kernels)], load_sem.at[1]),
        pltpu.make_async_copy(psf_h, psf, load_sem.at[2]),
    ]
    for h in range(2):
        home = plan.unit(owner, h, n - 1)
        for source, target in ((observed, obs), (weights, ivar)):
            loads.append(
                pltpu.make_async_copy(
                    source.at[pl.ds(home, m)], target.at[pl.ds(h * m, m)], load_sem.at[len(loads)]
                )
            )
    for load in loads:
        load.start()

    fill_tables(
        plan, per_dev, kernels, owner, strip, strips, inter, index, psf_index, table_v, tell_v
    )
    own_table = pltpu.make_async_copy(table_v, table, load_sem.at[7])
    own_table.start()
    pl.semaphore_wait(
        barrier, plan.bits + jnp.where(has[0], 1, 0) + jnp.where(has[1], 1, 0)
    )

    def tell_copy(up):
        return pltpu.make_async_remote_copy(
            src_ref=tell_v.at[up],
            dst_ref=told_v.at[1 - up],
            send_sem=tell_send.at[up],
            recv_sem=tell_recv.at[1 - up],
            device_id={"expo": strip + 2 * up - 1},
            device_id_type=MESH,
        )

    for up in range(2):

        @pl.when(has[up])
        def _(up=up):
            tell_copy(up).start()

    bank[kernels] = jnp.zeros(bank.shape[1:], bank.dtype)
    bank_t[kernels] = jnp.zeros(bank.shape[1:], bank.dtype)
    run[0] = jnp.zeros(run.shape[1:], run.dtype)
    loads[0].wait()
    for up in range(2):

        @pl.when(jnp.logical_not(has[up]))
        def _(up=up):
            told_v[up] = jnp.zeros(told_v.shape[1:], told_v.dtype)

            def wipe(i, carry):
                back[up * per_dev + i] = jnp.zeros(back.shape[1:], back.dtype)
                return carry

            lax.fori_loop(0, per_dev, wipe, 0)

        @pl.when(has[up])
        def _(up=up):
            tell_copy(1 - up).wait_recv()

    told_copy = pltpu.make_async_copy(told_v, told, load_sem.at[8])
    told_copy.start()
    told_copy.wait()

    def z_copy(up, q):
        where = up * per_dev + q * c
        return pltpu.make_async_remote_copy(
            src_ref=stage.at[pl.ds(where, c)],
            dst_ref=came.at[pl.ds(where, c)],
            send_sem=z_send.at[where // c],
            recv_sem=z_recv.at[where // c],
            device_id={"expo": strip + 2 * up - 1},
            device_id_type=MESH,
        )

    for q in range(pieces):
        for up in range(2):

            @pl.when(has[up])
            def _(up=up, q=q):
                def fill(i, carry):
                    stage[up * per_dev + q * c + i] = ready[per_dev + told[up, GIVE, q * c + i]]
                    return carry

                lax.fori_loop(0, c, fill, 0, unroll=2)
                z_copy(up, q).start()

    for load in loads[1:]:
        load.wait()

    turn_steps = n // 2 * plan.chunks * 2

    def turn_some(step):
        for source, target, count in ((bank, bank_t, kernels), (psf, psf_t, psf.shape[0])):

            def turn(i, carry, source=source, target=target):
                target[i] = source[i].T
                return carry

            lax.fori_loop(step * count // turn_steps, (step + 1) * count // turn_steps, turn, 0)

    own_table.wait()

    def take(q):
        for up in range(2):

            @pl.when(has[1 - up])
            def _(up=up):
                z_copy(up, q).wait_recv()

                def keep(i, carry):
                    a = q * c + i
                    ready[(1 - up) * 2 * per_dev + a] = came[up * per_dev + a]
                    return carry

                lax.fori_loop(0, c, keep, 0, unroll=2)

    def scatter_copy(h, t, k):
        where = plan.base(h, t) + k * c
        slot = where // c
        return pltpu.make_async_remote_copy(
            src_ref=terms.at[pl.ds(where, c)],
            dst_ref=got.at[pl.ds(where, c)],
            send_sem=rs_send.at[slot],
            recv_sem=rs_recv.at[slot],
            device_id={"scene": plan.partner(owner, h, plan.phase(t))},
            device_id_type=MESH,
        )

    def gather_copy(h, t, p, k):
        source = plan.base(h, t) + k * c
        target = plan.base(h, t - (n >> (p + 1))) + k * c
        slot = target // c
        return pltpu.make_async_remote_copy(
            src_ref=adj.at[pl.ds(source, c)],
            dst_ref=adj.at[pl.ds(target, c)],
            send_sem=ag_send.at[slot],
            recv_sem=ag_recv.at[slot],
            device_id={"scene": plan.partner(owner, h, p)},
            device_id_type=MESH,
        )

    def make_terms(h, t, k):
        where = plan.base(h, t) + k * c
        first = plan.unit(owner, h, t) + k * c

        def body(i, carry):
            at = [i * unroll + a for a in range(unroll)]
            inner = [
                dot(ready[table[READY, first + a]], bank[table[COL, first + a]], NT).astype(jnp.bfloat16)
                for a in at
            ]
            term = [dot(bank[table[ROW, first + a]], x, NN).astype(jnp.bfloat16) for a, x in zip(at, inner)]
            for a, x in zip(at, term):
                terms[where + a] = x
            return carry

        lax.fori_loop(0, c // unroll, body, 0)

    unroll = min(UNROLL, c)

    def arrived(t):
        return [t - (n >> (q + 1)) for q in range(plan.bits) if t >= n - (n >> (q + 1))]

    def summed(h, t, k, i):
        total = terms[plan.base(h, t) + k * c + i].astype(jnp.float32)
        for source in arrived(t):
            total = total + got[plan.base(h, source) + k * c + i].astype(jnp.float32)
        return total.astype(jnp.bfloat16)

    def pass_on(h, t, k):
        where = plan.base(h, t) + k * c

        def body(i, carry):
            terms[where + i] = summed(h, t, k, i)
            return carry

        lax.fori_loop(0, c, body, 0)

    def psf_pass(h, k):
        where = plan.base(h, n - 1) + k * c
        first = plan.unit(owner, h, n - 1) + k * c
        here = h * m + k * c

        def body(i, carry):
            at = [i * unroll + a for a in range(unroll)]
            which = [table[PSF, first + a] for a in at]
            half = [
                dot(summed(h, n - 1, k, a), psf[q], NT).astype(jnp.bfloat16) for a, q in zip(at, which)
            ]
            model = [dot(psf[q], x, NN) for q, x in zip(which, half)]
            weighted = [
                (ivar[here + a].astype(jnp.float32) * (x - obs[here + a].astype(jnp.float32))).astype(jnp.bfloat16)
                for a, x in zip(at, model)
            ]
            half = [dot(x, psf[q], NN).astype(jnp.bfloat16) for q, x in zip(which, weighted)]
            for a, q, x in zip(at, which, half):
                adj[where + a] = dot(psf_t[q], x, NN).astype(jnp.bfloat16)
            return carry

        lax.fori_loop(0, c // unroll, body, 0)

    for t in range(n):
        for k in range(plan.chunks):
            for h in range(2):
                q = (t * plan.chunks + k) * 2 + h
                if q < pieces:
                    take(q)
                make_terms(h, t, k)
                for source in arrived(t):
                    scatter_copy(h, source, k).wait_recv()
                if t < n // 2:
                    scatter_copy(h, t, k).start()
                    turn_some(q)
                elif t < n - 1:
                    pass_on(h, t, k)
                    scatter_copy(h, t, k).start()
                else:
                    psf_pass(h, k)
                    for p in reversed(range(plan.bits)):
                        gather_copy(h, n - 1, p, k).start()

    for up in range(2):

        @pl.when(has[up])
        def _(up=up):
            tell_copy(up).wait_send()
            for q in range(pieces):
                z_copy(up, q).wait_send()

    def back_copy(up, q):
        where = up * per_dev + q * c
        return pltpu.make_async_remote_copy(
            src_ref=leave.at[pl.ds(where, c)],
            dst_ref=back.at[pl.ds((1 - up) * per_dev + q * c, c)],
            send_sem=back_send.at[where // c],
            recv_sem=back_recv.at[((1 - up) * per_dev + q * c) // c],
            device_id={"expo": strip + 2 * up - 1},
            device_id_type=MESH,
        )

    def pull(h, t, k, turn):
        where = plan.base(h, t) + k * c
        first = plan.unit(owner, h, t) + k * c

        def body(i, carry):
            at = [i * unroll + a for a in range(unroll)]
            spread = [
                dot(adj[where + a], bank[table[COL, first + a]], NN).astype(jnp.bfloat16) for a in at
            ]
            pulled = [dot(bank_t[table[ROW, first + a]], x, NN) for a, x in zip(at, spread)]
            for a, x in zip(at, pulled):
                run[1 + turn + a] = x + run[table[PREV, first + a]]
            return carry

        lax.fori_loop(0, c // unroll, body, 0)

        for q in range(pieces):
            due = max(c, e - per_dev + (q + 1) * c)
            if turn < due <= turn + c:
                for up, last in ((0, LAST_LOW), (1, LAST_HIGH)):

                    @pl.when(has[up])
                    def _(up=up, last=last, q=q):
                        def put(i, carry):
                            a = q * c + i
                            leave[up * per_dev + a] = run[table[last, a]].astype(leave.dtype)
                            return carry

                        lax.fori_loop(0, c, put, 0, unroll=2)
                        back_copy(up, q).start()

    for units, start in plan.pulls():
        for k in range(plan.chunks):
            for at, t in enumerate(units):
                for h in range(2):
                    if t < n - 1:
                        last = plan.phase(t)
                        gather_copy(h, t + (n >> (last + 1)), last, k).wait_recv()
                        for p in reversed(range(last)):
                            gather_copy(h, t, p, k).start()
                    pull(h, t, k, ((start + k * len(units) + at) * 2 + h) * c)

    for t in range(n - 1):
        for k in range(plan.chunks):
            for h in range(2):
                scatter_copy(h, t, k).wait_send()
                p = plan.phase(t)
                gather_copy(h, t + (n >> (p + 1)), p, k).wait_send()

    for up in range(2):

        @pl.when(has[up])
        def _(up=up):
            for q in range(pieces):
                back_copy(1 - up, q).wait_recv()

    stores = []
    for q in range(pieces):

        def own(i, carry, q=q):
            b = q * c + i
            low = back[told[0, RANK, b]].astype(jnp.float32)
            high = back[per_dev + told[1, RANK, b]].astype(jnp.float32)
            out[b] = run[table[LAST_OWN, b]] + (low + high)
            return carry

        lax.fori_loop(0, c, own, 0, unroll=2)
        store = pltpu.make_async_copy(out.at[pl.ds(q * c, c)], out_h.at[pl.ds(q * c, c)], store_sem.at[q])
        store.start()
        stores.append(store)

    for up in range(2):

        @pl.when(has[up])
        def _(up=up):
            for q in range(pieces):
                back_copy(up, q).wait_send()

    for store in stores:
        store.wait()


def on_device(
    scene,
    observed,
    inverse_variance,
    intersection,
    resample_index,
    psf_index,
    resample_bank,
    psf_bank,
):
    per_dev, side = scene.shape[0], scene.shape[1:]
    e = intersection.shape[0]
    plan = Plan(lax.axis_size("scene"), e)
    slots = e // plan.c
    pieces = per_dev // plan.c
    kernels, psfs = resample_bank.shape[0], psf_bank.shape[0]
    dtype = scene.dtype
    vmem = pl.BlockSpec(memory_space=pltpu.VMEM)
    hbm = pl.BlockSpec(memory_space=pl.ANY)
    dma = pltpu.SemaphoreType.DMA
    blocks = lambda count, kind=dtype: pltpu.VMEM((count, *side), kind)
    return pl.pallas_call(
        functools.partial(gradient_kernel, plan, per_dev),
        out_shape=jax.ShapeDtypeStruct((per_dev, *side), jnp.float32),
        in_specs=[vmem] * 3 + [hbm] * 5,
        out_specs=hbm,
        scratch_shapes=[
            pltpu.VMEM((8, e), jnp.int32),
            pltpu.VMEM((2, 2, e), jnp.int32),
            pltpu.VMEM((2, 2, e), jnp.int32),
            pltpu.SMEM((8, e), jnp.int32),
            pltpu.SMEM((2, 2, e), jnp.int32),
            blocks(3 * per_dev),
            blocks(2 * per_dev),
            blocks(2 * per_dev),
            blocks(kernels + 1),
            blocks(kernels + 1),
            blocks(psfs),
            blocks(psfs),
            blocks(2 * plan.m),
            blocks(2 * plan.m),
            blocks(e),
            blocks(e),
            blocks(e),
            blocks(e + 1, jnp.float32),
            blocks(2 * per_dev),
            blocks(2 * per_dev),
            blocks(per_dev, jnp.float32),
            dma((9,)),
            dma((2,)),
            dma((2,)),
            dma((2 * pieces,)),
            dma((2 * pieces,)),
            dma((slots,)),
            dma((slots,)),
            dma((slots,)),
            dma((slots,)),
            dma((2 * pieces,)),
            dma((2 * pieces,)),
            dma((pieces,)),
        ],
        compiler_params=pltpu.CompilerParams(
            collective_id=0, has_side_effects=True, vmem_limit_bytes=VMEM_LIMIT
        ),
        name="gradient",
    )(
        intersection.T, resample_index.T, psf_index.reshape(1, e), scene, observed, inverse_variance,
        resample_bank, psf_bank,
    )


def solution(mesh):
    return jax.shard_map(
        on_device,
        mesh=mesh,
        in_specs=(
            P(("scene", "expo"), None, None),
            P("expo", None, None),
            P("expo", None, None),
            P("expo", None),
            P("expo", None),
            P("expo"),
            P(),
            P(),
        ),
        out_specs=P(("scene", "expo"), None, None),
        check_vma=False,
    )
```

```python
import functools

import jax
import jax.numpy as jnp
from jax import lax
from jax.experimental import pallas as pl
from jax.experimental.pallas import tpu as pltpu
from jax.sharding import PartitionSpec as P

MESH = pl.DeviceIdType.MESH
UNROLL = 4
CHUNK = 4
VMEM_LIMIT = 56 * 1024 * 1024

READY, ROW, COL, PREV, PSF, LAST_LOW, LAST_HIGH, LAST_OWN = range(8)
GIVE, RANK = range(2)


def dot(a, b, dims):
    return lax.dot_general(a, b, (dims, ((), ())), preferred_element_type=jnp.float32)


NN = ((1,), (0,))
NT = ((1,), (1,))


class Plan:
    def __init__(self, owners, exposures):
        self.n = owners
        self.bits = owners.bit_length() - 1
        assert 1 << self.bits == owners
        self.exposures = exposures
        self.half = exposures // 2
        self.m = self.half // owners
        self.c = min(CHUNK, self.m)
        self.chunks = self.m // self.c

    def bit(self, h, p):
        return p if h == 0 else self.bits - 1 - p

    def value(self, owner, h, p):
        return (owner // (1 << self.bit(h, p))) % 2

    def partner(self, owner, h, p):
        step = 1 << self.bit(h, p)
        return owner + step - 2 * step * self.value(owner, h, p)

    def unit(self, owner, h, t):
        u = 0
        for p in range(self.bits):
            weight = self.n >> (p + 1)
            v = self.value(owner, h, p)
            u = u + weight * (v if t & weight else 1 - v)
        return h * self.half + u * self.m

    def base(self, h, t):
        return h * self.half + t * self.m

    def hops(self, t):
        return 0 if t == self.n - 1 else 1 + self.hops(t + (self.n >> (self.phase(t) + 1)))

    def pulls(self):
        order, start = [], 0
        for hops in range(self.bits + 1):
            units = [t for t in reversed(range(self.n)) if self.hops(t) == hops]
            order.append((units, start))
            start += len(units) * self.chunks
        return order

    def turns(self, owner, j):
        h, u, i = j // self.half, j % self.half // self.m, j % self.m
        me = [(self.unit(owner, h, self.n - 1) - h * self.half) // self.m for h in range(2)]
        apart = jnp.bitwise_xor(u, jnp.where(h == 0, me[0], me[1]))
        k, i = i // self.c, i % self.c
        first = (((self.n - 1 - apart) * self.chunks + k) * 2 + h) * self.c + i
        place = jnp.zeros_like(j)
        for units, start in self.pulls():
            for at, t in enumerate(units):
                place = jnp.where(apart == self.n - 1 - t, start + k * len(units) + at, place)
        last = (place * 2 + h) * self.c + i
        return first, last

    def phase(self, t):
        p = 0
        while t >= self.n - (self.n >> (p + 1)):
            p += 1
        return p


def fill_tables(plan, per_dev, kernels, owner, strip, strips, inter, index, psf_index, table, tell):
    e, width = plan.exposures, inter.shape[0]
    where = inter[...]
    match = where // (strips * per_dev) == owner
    place = (where // per_dev % strips - strip + 1) * per_dev + where % per_dev

    def pick(values):
        return jnp.sum(jnp.where(match, values, 0), axis=0, keepdims=True)

    live = pick(jnp.ones_like(where)) > 0
    slot = jnp.where(live, jnp.clip(pick(place), 0, 3 * per_dev - 1), -1)
    kernel_of = index[...]
    table[pl.ds(ROW, 1), :] = jnp.where(live, pick(kernel_of[:width]), kernels)
    table[pl.ds(COL, 1), :] = pick(kernel_of[width:])
    table[pl.ds(PSF, 1), :] = psf_index[...]

    down = lax.broadcasted_iota(jnp.int32, (e, e), 0)
    along = lax.broadcasted_iota(jnp.int32, (e, e), 1)
    first_along, last_along = plan.turns(owner, along[:1])

    def upright(line):
        return jnp.sum(jnp.where(down == along, line, 0), axis=1, keepdims=True)

    def flat(column):
        return jnp.sum(jnp.where(down == along, column, 0), axis=0, keepdims=True)

    slot_down, last_down = upright(slot), upright(last_along)
    before = (slot_down == slot) & (last_down < last_along)
    table[pl.ds(PREV, 1), :] = jnp.max(jnp.where(before, last_down + 1, 0), axis=0, keepdims=True)

    ready = jnp.where(live, slot, per_dev)
    for side, last_row in ((0, LAST_LOW), (1, LAST_OWN), (2, LAST_HIGH)):
        near = slot - side * per_dev
        near = jnp.where((near >= 0) & (near < per_dev) & live, near, -1)
        hit = near == down
        last = jnp.max(jnp.where(hit, last_along + 1, 0), axis=1, keepdims=True)
        if side == 1:
            table[pl.ds(last_row, 1), :] = flat(last)
            continue
        line = down[:, :1]
        first = jnp.min(jnp.where(hit, first_along, e + down), axis=1, keepdims=True)
        rank = jnp.sum(jnp.where(flat(first) < first, 1, 0), axis=1, keepdims=True)
        give = jnp.sum(jnp.where(rank == along, down, 0), axis=0, keepdims=True)
        arrival = jnp.sum(jnp.where(hit, rank, 0), axis=0, keepdims=True)
        ready = jnp.where(near >= 0, side * per_dev + arrival, ready)
        order = jnp.where(line < per_dev, last, e + 1) * e + line
        order_along = flat(order)
        done = jnp.sum(jnp.where(order_along < order, 1, 0), axis=1, keepdims=True)
        table[pl.ds(last_row, 1), :] = jnp.sum(jnp.where(done == along, last, 0), axis=0, keepdims=True)
        up = side // 2
        tell[up, pl.ds(GIVE, 1), :] = jnp.clip(give, 0, per_dev - 1)
        tell[up, pl.ds(RANK, 1), :] = jnp.clip(flat(done), 0, per_dev - 1)
    table[pl.ds(READY, 1), :] = ready


def gradient_kernel(
    plan, per_dev, inter, index, psf_index, scene, observed, weights, bank_h, psf_h, out,
    table_v, tell_v, told_v, table, told, ready, stage, came, bank, bank_t, psf, psf_t, obs, ivar, terms, got,
    adj, run, leave, back, load_sem, tell_send, tell_recv, z_send, z_recv, rs_send, rs_recv, ag_send,
    ag_recv, back_send, back_recv,
):
    n, m, c = plan.n, plan.m, plan.c
    e = plan.exposures
    kernels = bank_h.shape[0]
    owner = lax.axis_index("scene")
    strip = lax.axis_index("expo")
    strips = lax.axis_size("expo")
    pieces = per_dev // c
    has = {0: strip > 0, 1: strip < strips - 1}

    barrier = pltpu.get_barrier_semaphore()
    for p in range(plan.bits):
        pl.semaphore_signal(
            barrier, inc=1, device_id={"scene": plan.partner(owner, 0, p)}, device_id_type=MESH
        )
    for up in range(2):

        @pl.when(has[up])
        def _(up=up):
            pl.semaphore_signal(
                barrier, inc=1, device_id={"expo": strip + 2 * up - 1}, device_id_type=MESH
            )

    loads = [
        pltpu.make_async_copy(scene, ready.at[pl.ds(per_dev, per_dev)], load_sem.at[0]),
        pltpu.make_async_copy(bank_h, bank.at[pl.ds(0, kernels)], load_sem.at[1]),
        pltpu.make_async_copy(psf_h, psf, load_sem.at[2]),
    ]
    for h in range(2):
        home = plan.unit(owner, h, n - 1)
        for source, target in ((observed, obs), (weights, ivar)):
            loads.append(
                pltpu.make_async_copy(
                    source.at[pl.ds(home, m)], target.at[pl.ds(h * m, m)], load_sem.at[len(loads)]
                )
            )
    for load in loads:
        load.start()

    fill_tables(
        plan, per_dev, kernels, owner, strip, strips, inter, index, psf_index, table_v, tell_v
    )
    own_table = pltpu.make_async_copy(table_v, table, load_sem.at[7])
    own_table.start()
    pl.semaphore_wait(
        barrier, plan.bits + jnp.where(has[0], 1, 0) + jnp.where(has[1], 1, 0)
    )

    def tell_copy(up):
        return pltpu.make_async_remote_copy(
            src_ref=tell_v.at[up],
            dst_ref=told_v.at[1 - up],
            send_sem=tell_send.at[up],
            recv_sem=tell_recv.at[1 - up],
            device_id={"expo": strip + 2 * up - 1},
            device_id_type=MESH,
        )

    for up in range(2):

        @pl.when(has[up])
        def _(up=up):
            tell_copy(up).start()

    bank[kernels] = jnp.zeros(bank.shape[1:], bank.dtype)
    bank_t[kernels] = jnp.zeros(bank.shape[1:], bank.dtype)
    run[0] = jnp.zeros(run.shape[1:], run.dtype)
    loads[0].wait()
    for up in range(2):

        @pl.when(jnp.logical_not(has[up]))
        def _(up=up):
            told_v[up] = jnp.zeros(told_v.shape[1:], told_v.dtype)

            def wipe(i, carry):
                back[up * per_dev + i] = jnp.zeros(back.shape[1:], back.dtype)
                return carry

            lax.fori_loop(0, per_dev, wipe, 0)

        @pl.when(has[up])
        def _(up=up):
            tell_copy(1 - up).wait_recv()

    told_copy = pltpu.make_async_copy(told_v, told, load_sem.at[8])
    told_copy.start()
    told_copy.wait()

    def z_copy(up, q):
        where = up * per_dev + q * c
        return pltpu.make_async_remote_copy(
            src_ref=stage.at[pl.ds(where, c)],
            dst_ref=came.at[pl.ds(where, c)],
            send_sem=z_send.at[where // c],
            recv_sem=z_recv.at[where // c],
            device_id={"expo": strip + 2 * up - 1},
            device_id_type=MESH,
        )

    for q in range(pieces):
        for up in range(2):

            @pl.when(has[up])
            def _(up=up, q=q):
                def fill(i, carry):
                    stage[up * per_dev + q * c + i] = ready[per_dev + told[up, GIVE, q * c + i]]
                    return carry

                lax.fori_loop(0, c, fill, 0, unroll=2)
                z_copy(up, q).start()

    for load in loads[1:]:
        load.wait()

    turn_steps = n // 2 * plan.chunks * 2

    def turn_some(step):
        for source, target, count in ((bank, bank_t, kernels), (psf, psf_t, psf.shape[0])):

            def turn(i, carry, source=source, target=target):
                target[i] = source[i].T
                return carry

            lax.fori_loop(step * count // turn_steps, (step + 1) * count // turn_steps, turn, 0)

    own_table.wait()

    def take(q):
        for up in range(2):

            @pl.when(has[1 - up])
            def _(up=up):
                z_copy(up, q).wait_recv()

                def keep(i, carry):
                    a = q * c + i
                    ready[(1 - up) * 2 * per_dev + a] = came[up * per_dev + a]
                    return carry

                lax.fori_loop(0, c, keep, 0, unroll=2)

    def scatter_copy(h, t, k):
        where = plan.base(h, t) + k * c
        slot = where // c
        return pltpu.make_async_remote_copy(
            src_ref=terms.at[pl.ds(where, c)],
            dst_ref=got.at[pl.ds(where, c)],
            send_sem=rs_send.at[slot],
            recv_sem=rs_recv.at[slot],
            device_id={"scene": plan.partner(owner, h, plan.phase(t))},
            device_id_type=MESH,
        )

    def gather_copy(h, t, p, k):
        source = plan.base(h, t) + k * c
        target = plan.base(h, t - (n >> (p + 1))) + k * c
        slot = target // c
        return pltpu.make_async_remote_copy(
            src_ref=adj.at[pl.ds(source, c)],
            dst_ref=adj.at[pl.ds(target, c)],
            send_sem=ag_send.at[slot],
            recv_sem=ag_recv.at[slot],
            device_id={"scene": plan.partner(owner, h, p)},
            device_id_type=MESH,
        )

    def make_terms(h, t, k):
        where = plan.base(h, t) + k * c
        first = plan.unit(owner, h, t) + k * c

        def body(i, carry):
            at = [i * unroll + a for a in range(unroll)]
            inner = [
                dot(ready[table[READY, first + a]], bank[table[COL, first + a]], NT).astype(jnp.bfloat16)
                for a in at
            ]
            term = [dot(bank[table[ROW, first + a]], x, NN).astype(jnp.bfloat16) for a, x in zip(at, inner)]
            for a, x in zip(at, term):
                terms[where + a] = x
            return carry

        lax.fori_loop(0, c // unroll, body, 0)

    unroll = min(UNROLL, c)

    def arrived(t):
        return [t - (n >> (q + 1)) for q in range(plan.bits) if t >= n - (n >> (q + 1))]

    def summed(h, t, k, i):
        total = terms[plan.base(h, t) + k * c + i].astype(jnp.float32)
        for source in arrived(t):
            total = total + got[plan.base(h, source) + k * c + i].astype(jnp.float32)
        return total.astype(jnp.bfloat16)

    def pass_on(h, t, k):
        where = plan.base(h, t) + k * c

        def body(i, carry):
            terms[where + i] = summed(h, t, k, i)
            return carry

        lax.fori_loop(0, c, body, 0)

    def psf_pass(h, k):
        where = plan.base(h, n - 1) + k * c
        first = plan.unit(owner, h, n - 1) + k * c
        here = h * m + k * c

        def body(i, carry):
            at = [i * unroll + a for a in range(unroll)]
            which = [table[PSF, first + a] for a in at]
            half = [
                dot(summed(h, n - 1, k, a), psf[q], NT).astype(jnp.bfloat16) for a, q in zip(at, which)
            ]
            model = [dot(psf[q], x, NN) for q, x in zip(which, half)]
            weighted = [
                (ivar[here + a].astype(jnp.float32) * (x - obs[here + a].astype(jnp.float32))).astype(jnp.bfloat16)
                for a, x in zip(at, model)
            ]
            half = [dot(x, psf[q], NN).astype(jnp.bfloat16) for q, x in zip(which, weighted)]
            for a, q, x in zip(at, which, half):
                adj[where + a] = dot(psf_t[q], x, NN).astype(jnp.bfloat16)
            return carry

        lax.fori_loop(0, c // unroll, body, 0)

    for t in range(n):
        for k in range(plan.chunks):
            for h in range(2):
                q = (t * plan.chunks + k) * 2 + h
                if q < pieces:
                    take(q)
                make_terms(h, t, k)
                for source in arrived(t):
                    scatter_copy(h, source, k).wait_recv()
                if t < n // 2:
                    scatter_copy(h, t, k).start()
                    turn_some(q)
                elif t < n - 1:
                    pass_on(h, t, k)
                    scatter_copy(h, t, k).start()
                else:
                    psf_pass(h, k)
                    for p in reversed(range(plan.bits)):
                        gather_copy(h, n - 1, p, k).start()

    for up in range(2):

        @pl.when(has[up])
        def _(up=up):
            tell_copy(up).wait_send()
            for q in range(pieces):
                z_copy(up, q).wait_send()

    def back_copy(up, q):
        where = up * per_dev + q * c
        return pltpu.make_async_remote_copy(
            src_ref=leave.at[pl.ds(where, c)],
            dst_ref=back.at[pl.ds((1 - up) * per_dev + q * c, c)],
            send_sem=back_send.at[where // c],
            recv_sem=back_recv.at[((1 - up) * per_dev + q * c) // c],
            device_id={"expo": strip + 2 * up - 1},
            device_id_type=MESH,
        )

    def pull(h, t, k, turn):
        where = plan.base(h, t) + k * c
        first = plan.unit(owner, h, t) + k * c

        def body(i, carry):
            at = [i * unroll + a for a in range(unroll)]
            spread = [
                dot(adj[where + a], bank[table[COL, first + a]], NN).astype(jnp.bfloat16) for a in at
            ]
            pulled = [dot(bank_t[table[ROW, first + a]], x, NN) for a, x in zip(at, spread)]
            for a, x in zip(at, pulled):
                run[1 + turn + a] = x + run[table[PREV, first + a]]
            return carry

        lax.fori_loop(0, c // unroll, body, 0)

        for q in range(pieces):
            due = max(c, e - per_dev + (q + 1) * c)
            if turn < due <= turn + c:
                for up, last in ((0, LAST_LOW), (1, LAST_HIGH)):

                    @pl.when(has[up])
                    def _(up=up, last=last, q=q):
                        def put(i, carry):
                            a = q * c + i
                            leave[up * per_dev + a] = run[table[last, a]].astype(leave.dtype)
                            return carry

                        lax.fori_loop(0, c, put, 0, unroll=2)
                        back_copy(up, q).start()

    for units, start in plan.pulls():
        for k in range(plan.chunks):
            for at, t in enumerate(units):
                for h in range(2):
                    if t < n - 1:
                        last = plan.phase(t)
                        gather_copy(h, t + (n >> (last + 1)), last, k).wait_recv()
                        for p in reversed(range(last)):
                            gather_copy(h, t, p, k).start()
                    pull(h, t, k, ((start + k * len(units) + at) * 2 + h) * c)

    for t in range(n - 1):
        for k in range(plan.chunks):
            for h in range(2):
                scatter_copy(h, t, k).wait_send()
                p = plan.phase(t)
                gather_copy(h, t + (n >> (p + 1)), p, k).wait_send()

    for up in range(2):

        @pl.when(has[up])
        def _(up=up):
            for q in range(pieces):
                back_copy(1 - up, q).wait_recv()

    for q in range(pieces):

        def own(i, carry, q=q):
            b = q * c + i
            low = back[told[0, RANK, b]].astype(jnp.float32)
            high = back[per_dev + told[1, RANK, b]].astype(jnp.float32)
            out[b] = run[table[LAST_OWN, b]] + (low + high)
            return carry

        lax.fori_loop(0, c, own, 0, unroll=2)

    for up in range(2):

        @pl.when(has[up])
        def _(up=up):
            for q in range(pieces):
                back_copy(up, q).wait_send()


def on_device(
    scene,
    observed,
    inverse_variance,
    intersection,
    resample_index,
    psf_index,
    resample_bank,
    psf_bank,
):
    per_dev, side = scene.shape[0], scene.shape[1:]
    e = intersection.shape[0]
    plan = Plan(lax.axis_size("scene"), e)
    slots = e // plan.c
    pieces = per_dev // plan.c
    kernels, psfs = resample_bank.shape[0], psf_bank.shape[0]
    dtype = scene.dtype
    vmem = pl.BlockSpec(memory_space=pltpu.VMEM)
    hbm = pl.BlockSpec(memory_space=pl.ANY)
    dma = pltpu.SemaphoreType.DMA
    blocks = lambda count, kind=dtype: pltpu.VMEM((count, *side), kind)
    return pl.pallas_call(
        functools.partial(gradient_kernel, plan, per_dev),
        out_shape=pltpu.VMEM((per_dev, *side), jnp.float32),
        in_specs=[vmem] * 3 + [hbm] * 5,
        out_specs=pl.BlockSpec(memory_space=pltpu.VMEM),
        scratch_shapes=[
            pltpu.VMEM((8, e), jnp.int32),
            pltpu.VMEM((2, 2, e), jnp.int32),
            pltpu.VMEM((2, 2, e), jnp.int32),
            pltpu.SMEM((8, e), jnp.int32),
            pltpu.SMEM((2, 2, e), jnp.int32),
            blocks(3 * per_dev),
            blocks(2 * per_dev),
            blocks(2 * per_dev),
            blocks(kernels + 1),
            blocks(kernels + 1),
            blocks(psfs),
            blocks(psfs),
            blocks(2 * plan.m),
            blocks(2 * plan.m),
            blocks(e),
            blocks(e),
            blocks(e),
            blocks(e + 1, jnp.float32),
            blocks(2 * per_dev),
            blocks(2 * per_dev),
            dma((9,)),
            dma((2,)),
            dma((2,)),
            dma((2 * pieces,)),
            dma((2 * pieces,)),
            dma((slots,)),
            dma((slots,)),
            dma((slots,)),
            dma((slots,)),
            dma((2 * pieces,)),
            dma((2 * pieces,)),
        ],
        compiler_params=pltpu.CompilerParams(
            collective_id=0, has_side_effects=True, vmem_limit_bytes=VMEM_LIMIT
        ),
        name="gradient",
    )(
        intersection.T, resample_index.T, psf_index.reshape(1, e), scene, observed, inverse_variance,
        resample_bank, psf_bank,
    )


def solution(mesh):
    return jax.shard_map(
        on_device,
        mesh=mesh,
        in_specs=(
            P(("scene", "expo"), None, None),
            P("expo", None, None),
            P("expo", None, None),
            P("expo", None),
            P("expo", None),
            P("expo"),
            P(),
            P(),
        ),
        out_specs=P(("scene", "expo"), None, None),
        check_vma=False,
    )
```

```python
import functools

import jax
import jax.numpy as jnp
from jax import lax
from jax.experimental import pallas as pl
from jax.experimental.pallas import tpu as pltpu
from jax.sharding import PartitionSpec as P

MESH = pl.DeviceIdType.MESH
CHUNK = 2
HOP = 4
VMEM_LIMIT = 56 * 1024 * 1024

READY, ROW, COL, PREV, PSF, LAST_LOW, LAST_HIGH, LAST_OWN = range(8)
GIVE, RANK = range(2)


def dot(a, b, dims):
    return lax.dot_general(a, b, (dims, ((), ())), preferred_element_type=jnp.float32)


NN = ((1,), (0,))
NT = ((1,), (1,))


class Plan:
    def __init__(self, owners, exposures):
        self.n = owners
        self.bits = owners.bit_length() - 1
        assert 1 << self.bits == owners
        self.exposures = exposures
        self.half = exposures // 2
        self.m = self.half // owners
        self.c = min(CHUNK, self.m)
        self.chunks = self.m // self.c
        self.home = owners - 1
        self.events = self.schedule()
        self.made, self.pulled = [], []
        for kind, stage, k in self.events:
            if kind != "gather":
                self.made += [(h, t, k) for h in range(2) for t in self.sent(stage)]
            if kind != "scatter":
                self.pulled += [(h, t, k) for t in self.reached(stage) for h in range(2)]

    def bit(self, h, p):
        return p if h == 0 else self.bits - 1 - p

    def value(self, owner, h, p):
        return (owner // (1 << self.bit(h, p))) % 2

    def partner(self, owner, h, p):
        step = 1 << self.bit(h, p)
        return owner + step - 2 * step * self.value(owner, h, p)

    def unit(self, owner, h, t):
        u = 0
        for p in range(self.bits):
            weight = self.n >> (p + 1)
            v = self.value(owner, h, p)
            u = u + weight * (v if t & weight else 1 - v)
        return h * self.half + u * self.m

    def base(self, h, t, k):
        return h * self.half + (k * self.n + t) * self.c

    def phase(self, t):
        p = 0
        while t >= self.n - (self.n >> (p + 1)):
            p += 1
        return p

    def sent(self, p):
        if p >= self.bits:
            return [self.home]
        return list(range(self.n - (self.n >> p), self.n - (self.n >> (p + 1))))

    def hops(self, t):
        return 0 if t == self.home else 1 + self.hops(t + (self.n >> (self.phase(t) + 1)))

    def reached(self, stage):
        return [t for t in reversed(range(self.n)) if self.hops(t) == stage - self.bits]

    def schedule(self):
        bits, events = self.bits, []
        for i in range(self.chunks + 2 * bits):
            step = [("scatter", p, i - p) for p in reversed(range(1, bits))]
            step += [("scatter", 0, i), ("gather", bits + 1, i - bits), ("home", bits, i - bits + 1)]
            step += [("gather", bits + d, i - bits - d + 2) for d in range(2, bits + 1)]
            events += [event for event in step if 0 <= event[2] < self.chunks]
        return events

    def turns(self, owner, j):
        h, u, i = j // self.half, j % self.half // self.m, j % self.m
        me = [(self.unit(owner, h, self.home) - h * self.half) // self.m for h in range(2)]
        apart = jnp.bitwise_xor(u, jnp.where(h == 0, me[0], me[1]))
        k, i = i // self.c, i % self.c
        which = ((self.home - apart) * self.chunks + k) * 2 + h
        found = []
        for order in (self.made, self.pulled):
            place = jnp.zeros_like(j)
            for at, (h, t, k) in enumerate(order):
                place = jnp.where(which == (t * self.chunks + k) * 2 + h, at, place)
            found.append(place * self.c + i)
        return found


def fill_tables(plan, per_dev, kernels, owner, strip, strips, inter, index, psf_index, table, tell):
    e, width = plan.exposures, inter.shape[0]
    where = inter[...]
    match = where // (strips * per_dev) == owner
    place = (where // per_dev % strips - strip + 1) * per_dev + where % per_dev

    def pick(values):
        return jnp.sum(jnp.where(match, values, 0), axis=0, keepdims=True)

    live = pick(jnp.ones_like(where)) > 0
    slot = jnp.where(live, jnp.clip(pick(place), 0, 3 * per_dev - 1), -1)
    kernel_of = index[...]
    table[pl.ds(ROW, 1), :] = jnp.where(live, pick(kernel_of[:width]), kernels)
    table[pl.ds(COL, 1), :] = pick(kernel_of[width:])
    table[pl.ds(PSF, 1), :] = psf_index[...]

    down = lax.broadcasted_iota(jnp.int32, (e, e), 0)
    along = lax.broadcasted_iota(jnp.int32, (e, e), 1)
    first_along, last_along = plan.turns(owner, along[:1])

    def upright(line):
        return jnp.sum(jnp.where(down == along, line, 0), axis=1, keepdims=True)

    def flat(column):
        return jnp.sum(jnp.where(down == along, column, 0), axis=0, keepdims=True)

    slot_down, last_down = upright(slot), upright(last_along)
    before = (slot_down == slot) & (last_down < last_along)
    table[pl.ds(PREV, 1), :] = jnp.max(jnp.where(before, last_down + 1, 0), axis=0, keepdims=True)

    ready = jnp.where(live, slot, per_dev)
    for side, last_row in ((0, LAST_LOW), (1, LAST_OWN), (2, LAST_HIGH)):
        near = slot - side * per_dev
        near = jnp.where((near >= 0) & (near < per_dev) & live, near, -1)
        hit = near == down
        last = jnp.max(jnp.where(hit, last_along + 1, 0), axis=1, keepdims=True)
        if side == 1:
            table[pl.ds(last_row, 1), :] = flat(last)
            continue
        line = down[:, :1]
        first = jnp.min(jnp.where(hit, first_along, e + down), axis=1, keepdims=True)
        rank = jnp.sum(jnp.where(flat(first) < first, 1, 0), axis=1, keepdims=True)
        give = jnp.sum(jnp.where(rank == along, down, 0), axis=0, keepdims=True)
        arrival = jnp.sum(jnp.where(hit, rank, 0), axis=0, keepdims=True)
        ready = jnp.where(near >= 0, side * per_dev + arrival, ready)
        order = jnp.where(line < per_dev, last, e + 1) * e + line
        order_along = flat(order)
        done = jnp.sum(jnp.where(order_along < order, 1, 0), axis=1, keepdims=True)
        table[pl.ds(last_row, 1), :] = jnp.sum(jnp.where(done == along, last, 0), axis=0, keepdims=True)
        up = side // 2
        tell[up, pl.ds(GIVE, 1), :] = jnp.clip(give, 0, per_dev - 1)
        tell[up, pl.ds(RANK, 1), :] = jnp.clip(flat(done), 0, per_dev - 1)
    table[pl.ds(READY, 1), :] = ready


def gradient_kernel(
    plan, per_dev, inter, index, psf_index, scene, observed, weights, bank_h, psf_h, out,
    table_v, tell_v, told_v, table, told, ready, stage, came, bank, bank_t, psf, psf_t, obs, ivar, terms, got,
    adj, run, leave, back, load_sem, tell_send, tell_recv, z_send, z_recv, rs_send, rs_recv, ag_send,
    ag_recv, back_send, back_recv,
):
    n, m, c, home = plan.n, plan.m, plan.c, plan.home
    e = plan.exposures
    kernels = bank_h.shape[0]
    owner = lax.axis_index("scene")
    strip = lax.axis_index("expo")
    strips = lax.axis_size("expo")
    z = min(HOP, per_dev)
    pieces = per_dev // z
    has = {0: strip > 0, 1: strip < strips - 1}

    barrier = pltpu.get_barrier_semaphore()
    for p in range(plan.bits):
        pl.semaphore_signal(
            barrier, inc=1, device_id={"scene": plan.partner(owner, 0, p)}, device_id_type=MESH
        )
    for up in range(2):

        @pl.when(has[up])
        def _(up=up):
            pl.semaphore_signal(
                barrier, inc=1, device_id={"expo": strip + 2 * up - 1}, device_id_type=MESH
            )

    loads = [
        pltpu.make_async_copy(scene, ready.at[pl.ds(per_dev, per_dev)], load_sem.at[0]),
        pltpu.make_async_copy(bank_h, bank.at[pl.ds(0, kernels)], load_sem.at[1]),
        pltpu.make_async_copy(psf_h, psf, load_sem.at[2]),
    ]
    for h in range(2):
        start = plan.unit(owner, h, home)
        for source, target in ((observed, obs), (weights, ivar)):
            loads.append(
                pltpu.make_async_copy(
                    source.at[pl.ds(start, m)], target.at[pl.ds(h * m, m)], load_sem.at[len(loads)]
                )
            )
    for load in loads:
        load.start()

    fill_tables(
        plan, per_dev, kernels, owner, strip, strips, inter, index, psf_index, table_v, tell_v
    )
    own_table = pltpu.make_async_copy(table_v, table, load_sem.at[7])
    own_table.start()
    pl.semaphore_wait(
        barrier, plan.bits + jnp.where(has[0], 1, 0) + jnp.where(has[1], 1, 0)
    )

    def tell_copy(up):
        return pltpu.make_async_remote_copy(
            src_ref=tell_v.at[up],
            dst_ref=told_v.at[1 - up],
            send_sem=tell_send.at[up],
            recv_sem=tell_recv.at[1 - up],
            device_id={"expo": strip + 2 * up - 1},
            device_id_type=MESH,
        )

    for up in range(2):

        @pl.when(has[up])
        def _(up=up):
            tell_copy(up).start()

    bank[kernels] = jnp.zeros(bank.shape[1:], bank.dtype)
    bank_t[kernels] = jnp.zeros(bank.shape[1:], bank.dtype)
    run[0] = jnp.zeros(run.shape[1:], run.dtype)
    loads[0].wait()
    for up in range(2):

        @pl.when(jnp.logical_not(has[up]))
        def _(up=up):
            told_v[up] = jnp.zeros(told_v.shape[1:], told_v.dtype)

            def wipe(i, carry):
                back[up * per_dev + i] = jnp.zeros(back.shape[1:], back.dtype)
                return carry

            lax.fori_loop(0, per_dev, wipe, 0)

        @pl.when(has[up])
        def _(up=up):
            tell_copy(1 - up).wait_recv()

    told_copy = pltpu.make_async_copy(told_v, told, load_sem.at[8])
    told_copy.start()
    told_copy.wait()

    def z_copy(up, q):
        where = up * per_dev + q * z
        return pltpu.make_async_remote_copy(
            src_ref=stage.at[pl.ds(where, z)],
            dst_ref=came.at[pl.ds(where, z)],
            send_sem=z_send.at[where // z],
            recv_sem=z_recv.at[where // z],
            device_id={"expo": strip + 2 * up - 1},
            device_id_type=MESH,
        )

    for q in range(pieces):
        for up in range(2):

            @pl.when(has[up])
            def _(up=up, q=q):
                for i in range(q * z, (q + 1) * z):
                    stage[up * per_dev + i] = ready[per_dev + told[up, GIVE, i]]
                z_copy(up, q).start()

    for load in loads[1:]:
        load.wait()

    def turn_all(source, target, count):
        def turn(i, carry):
            target[i] = source[i].T
            return carry

        lax.fori_loop(0, count, turn, 0)

    own_table.wait()
    taken, made, pulled = [0], [0], [0]

    def take(turns):
        while taken[0] < min(turns, per_dev):
            q = taken[0] // z
            taken[0] += z
            for up in range(2):

                @pl.when(has[1 - up])
                def _(up=up, q=q):
                    z_copy(up, q).wait_recv()
                    for i in range(q * z, (q + 1) * z):
                        ready[(1 - up) * 2 * per_dev + i] = came[up * per_dev + i]

    def scatter_copy(h, p, k):
        units = plan.sent(p)
        where, count = plan.base(h, units[0], k), len(units) * c
        slot = (k * 2 + h) * plan.bits + p
        return pltpu.make_async_remote_copy(
            src_ref=terms.at[pl.ds(where, count)],
            dst_ref=got.at[pl.ds(where, count)],
            send_sem=rs_send.at[slot],
            recv_sem=rs_recv.at[slot],
            device_id={"scene": plan.partner(owner, h, p)},
            device_id_type=MESH,
        )

    def gather_copy(h, t, p, k):
        source = plan.base(h, t, k)
        target = plan.base(h, t - (n >> (p + 1)), k)
        slot = target // c
        return pltpu.make_async_remote_copy(
            src_ref=adj.at[pl.ds(source, c)],
            dst_ref=adj.at[pl.ds(target, c)],
            send_sem=ag_send.at[slot],
            recv_sem=ag_recv.at[slot],
            device_id={"scene": plan.partner(owner, h, p)},
            device_id_type=MESH,
        )

    def spots(h, t, k):
        first = plan.unit(owner, h, t) + k * c
        return [(plan.base(h, t, k) + i, first + i) for i in range(c)]

    def make_terms(chunks):
        made[0] += len(chunks) * c
        take(made[0])
        at = [spot for chunk in chunks for spot in spots(*chunk)]
        inner = [dot(ready[table[READY, j]], bank[table[COL, j]], NT).astype(jnp.bfloat16) for _, j in at]
        term = [dot(bank[table[ROW, j]], x, NN).astype(jnp.bfloat16) for (_, j), x in zip(at, inner)]
        for (where, _), x in zip(at, term):
            terms[where] = x

    def summed(h, t, k, i):
        total = terms[plan.base(h, t, k) + i].astype(jnp.float32)
        for p in range(plan.phase(t)):
            total = total + got[plan.base(h, t - (n >> (p + 1)), k) + i].astype(jnp.float32)
        return total.astype(jnp.bfloat16)

    def scatter(p, k):
        units = plan.sent(p)
        if k > 0 or p > 0:
            make_terms([(h, t, k) for h in range(2) for t in units])
        for h in range(2):
            if k == p == 0:
                make_terms([(h, t, k) for t in units])
            if p > 0:
                scatter_copy(h, p - 1, k).wait_recv()
                for t in units:
                    for i in range(c):
                        terms[plan.base(h, t, k) + i] = summed(h, t, k, i)
            scatter_copy(h, p, k).start()

    def come_home(k):
        make_terms([(h, home, k) for h in range(2)])
        for h in range(2):
            scatter_copy(h, plan.bits - 1, k).wait_recv()
        at = [(h, i) for h in range(2) for i in range(c)]
        which = [table[PSF, plan.unit(owner, h, home) + k * c + i] for h, i in at]
        half = [dot(summed(h, home, k, i), psf[q], NT).astype(jnp.bfloat16) for (h, i), q in zip(at, which)]
        model = [dot(psf[q], x, NN) for q, x in zip(which, half)]
        weighted = []
        for (h, i), x in zip(at, model):
            here = h * m + k * c + i
            x = ivar[here].astype(jnp.float32) * (x - obs[here].astype(jnp.float32))
            weighted.append(x.astype(jnp.bfloat16))
        half = [dot(x, psf[q], NN).astype(jnp.bfloat16) for q, x in zip(which, weighted)]
        for (h, i), q, x in zip(at, which, half):
            adj[plan.base(h, home, k) + i] = dot(psf_t[q], x, NN).astype(jnp.bfloat16)
        for p in reversed(range(plan.bits)):
            for h in range(2):
                gather_copy(h, home, p, k).start()

    def back_copy(up, q):
        where = up * per_dev + q * z
        there = (1 - up) * per_dev + q * z
        return pltpu.make_async_remote_copy(
            src_ref=leave.at[pl.ds(where, z)],
            dst_ref=back.at[pl.ds(there, z)],
            send_sem=back_send.at[where // z],
            recv_sem=back_recv.at[there // z],
            device_id={"expo": strip + 2 * up - 1},
            device_id_type=MESH,
        )

    def pull(chunks):
        at = [spot for chunk in chunks for spot in spots(*chunk)]
        spread = [dot(adj[where], bank[table[COL, j]], NN).astype(jnp.bfloat16) for where, j in at]
        moved = [dot(bank_t[table[ROW, j]], x, NN) for (_, j), x in zip(at, spread)]
        before = pulled[0]
        for i, ((_, j), x) in enumerate(zip(at, moved)):
            run[1 + before + i] = x + run[table[PREV, j]]
        pulled[0] += len(at)

        for q in range(pieces):
            if before < max(1, e - per_dev + (q + 1) * z) <= pulled[0]:
                for up, last in ((0, LAST_LOW), (1, LAST_HIGH)):

                    @pl.when(has[up])
                    def _(up=up, last=last, q=q):
                        for i in range(q * z, (q + 1) * z):
                            leave[up * per_dev + i] = run[table[last, i]].astype(leave.dtype)
                        back_copy(up, q).start()

    for number, (kind, at_stage, k) in enumerate(plan.events):
        if kind == "scatter":
            scatter(at_stage, k)
            if number == 0:
                turn_all(psf, psf_t, psf.shape[0])
        elif kind == "home":
            if k == 0:
                turn_all(bank, bank_t, kernels)
            come_home(k)
            pull([(h, home, k) for h in range(2)])
        else:
            chunks = [(h, t, k) for t in plan.reached(at_stage) for h in range(2)]
            for h, t, _ in chunks:
                last = plan.phase(t)
                gather_copy(h, t + (n >> (last + 1)), last, k).wait_recv()
                for p in reversed(range(last)):
                    gather_copy(h, t, p, k).start()
            pull(chunks)

    for k in range(plan.chunks):
        for h in range(2):
            for p in range(plan.bits):
                scatter_copy(h, p, k).wait_send()
            for t in range(home):
                p = plan.phase(t)
                gather_copy(h, t + (n >> (p + 1)), p, k).wait_send()

    for up in range(2):

        @pl.when(has[up])
        def _(up=up):
            tell_copy(up).wait_send()
            for q in range(pieces):
                z_copy(up, q).wait_send()

    for up in range(2):

        @pl.when(has[up])
        def _(up=up):
            for q in range(pieces):
                back_copy(1 - up, q).wait_recv()

    def own(b, carry):
        low = back[told[0, RANK, b]].astype(jnp.float32)
        high = back[per_dev + told[1, RANK, b]].astype(jnp.float32)
        out[b] = run[table[LAST_OWN, b]] + (low + high)
        return carry

    lax.fori_loop(0, per_dev, own, 0, unroll=4)

    for up in range(2):

        @pl.when(has[up])
        def _(up=up):
            for q in range(pieces):
                back_copy(up, q).wait_send()


def on_device(
    scene,
    observed,
    inverse_variance,
    intersection,
    resample_index,
    psf_index,
    resample_bank,
    psf_bank,
):
    per_dev, side = scene.shape[0], scene.shape[1:]
    e = intersection.shape[0]
    plan = Plan(lax.axis_size("scene"), e)
    slots = e // plan.c
    pieces = per_dev // min(HOP, per_dev)
    kernels, psfs = resample_bank.shape[0], psf_bank.shape[0]
    dtype = scene.dtype
    vmem = pl.BlockSpec(memory_space=pltpu.VMEM)
    hbm = pl.BlockSpec(memory_space=pl.ANY)
    dma = pltpu.SemaphoreType.DMA
    blocks = lambda count, kind=dtype: pltpu.VMEM((count, *side), kind)
    return pl.pallas_call(
        functools.partial(gradient_kernel, plan, per_dev),
        out_shape=pltpu.VMEM((per_dev, *side), jnp.float32),
        in_specs=[vmem] * 3 + [hbm] * 5,
        out_specs=pl.BlockSpec(memory_space=pltpu.VMEM),
        scratch_shapes=[
            pltpu.VMEM((8, e), jnp.int32),
            pltpu.VMEM((2, 2, e), jnp.int32),
            pltpu.VMEM((2, 2, e), jnp.int32),
            pltpu.SMEM((8, e), jnp.int32),
            pltpu.SMEM((2, 2, e), jnp.int32),
            blocks(3 * per_dev),
            blocks(2 * per_dev),
            blocks(2 * per_dev),
            blocks(kernels + 1),
            blocks(kernels + 1),
            blocks(psfs),
            blocks(psfs),
            blocks(2 * plan.m),
            blocks(2 * plan.m),
            blocks(e),
            blocks(e),
            blocks(e),
            blocks(e + 1, jnp.float32),
            blocks(2 * per_dev),
            blocks(2 * per_dev),
            dma((9,)),
            dma((2,)),
            dma((2,)),
            dma((2 * pieces,)),
            dma((2 * pieces,)),
            dma((2 * plan.chunks * plan.bits,)),
            dma((2 * plan.chunks * plan.bits,)),
            dma((slots,)),
            dma((slots,)),
            dma((2 * pieces,)),
            dma((2 * pieces,)),
        ],
        compiler_params=pltpu.CompilerParams(
            collective_id=0, has_side_effects=True, vmem_limit_bytes=VMEM_LIMIT
        ),
        name="gradient",
    )(
        intersection.T, resample_index.T, psf_index.reshape(1, e), scene, observed, inverse_variance,
        resample_bank, psf_bank,
    )


def solution(mesh):
    return jax.shard_map(
        on_device,
        mesh=mesh,
        in_specs=(
            P(("scene", "expo"), None, None),
            P("expo", None, None),
            P("expo", None, None),
            P("expo", None),
            P("expo", None),
            P("expo"),
            P(),
            P(),
        ),
        out_specs=P(("scene", "expo"), None, None),
        check_vma=False,
    )
```

```python
import functools

import jax
import jax.numpy as jnp
from jax import lax
from jax.experimental import pallas as pl
from jax.experimental.pallas import tpu as pltpu
from jax.sharding import PartitionSpec as P

MESH = pl.DeviceIdType.MESH
CHUNK = 4
EDGE = 2
VMEM_LIMIT = 56 * 1024 * 1024

READY, ROW, COL, PREV, PSF, LAST_LOW, LAST_HIGH, LAST_OWN = range(8)
GIVE, RANK = range(2)


def dot(a, b, dims):
    return lax.dot_general(a, b, (dims, ((), ())), preferred_element_type=jnp.float32)


NN = ((1,), (0,))
NT = ((1,), (1,))


def cut(length, first, last):
    sizes = [min(first, length)]
    while sum(sizes) < length:
        rest = length - sum(sizes)
        sizes.append(min(CHUNK, rest - last) if rest > last else rest)
    return [(sum(sizes[:i]), size) for i, size in enumerate(sizes)]


class Plan:
    def __init__(self, owners, exposures):
        self.n = owners
        self.bits = owners.bit_length() - 1
        assert 1 << self.bits == owners
        self.exposures = exposures
        self.half = exposures // 2
        self.m = self.half // owners
        self.cuts = cut(self.m, EDGE, EDGE)
        self.chunks = len(self.cuts)
        self.made, self.pulled = [], []
        for t in range(self.n):
            self.made += [(h, t, k) for k in range(self.chunks) for h in range(2)]
        for hops in range(self.bits + 1):
            units = [t for t in reversed(range(self.n)) if self.hops(t) == hops]
            self.pulled += [(h, t, k) for k in range(self.chunks) for t in units for h in range(2)]

    def bit(self, h, p):
        return p if h == 0 else self.bits - 1 - p

    def value(self, owner, h, p):
        return (owner // (1 << self.bit(h, p))) % 2

    def partner(self, owner, h, p):
        step = 1 << self.bit(h, p)
        return owner + step - 2 * step * self.value(owner, h, p)

    def unit(self, owner, h, t):
        u = 0
        for p in range(self.bits):
            weight = self.n >> (p + 1)
            v = self.value(owner, h, p)
            u = u + weight * (v if t & weight else 1 - v)
        return h * self.half + u * self.m

    def base(self, h, t):
        return h * self.half + t * self.m

    def hops(self, t):
        return 0 if t == self.n - 1 else 1 + self.hops(t + (self.n >> (self.phase(t) + 1)))

    def turn(self, order, chunk):
        return sum(self.cuts[k][1] for _, _, k in order[: order.index(chunk)])

    def turns(self, owner, j):
        h, u, i = j // self.half, j % self.half // self.m, j % self.m
        me = [(self.unit(owner, h, self.n - 1) - h * self.half) // self.m for h in range(2)]
        t = self.n - 1 - jnp.bitwise_xor(u, jnp.where(h == 0, me[0], me[1]))
        found = []
        for order in (self.made, self.pulled):
            place = jnp.zeros_like(j)
            for chunk in order:
                start, size = self.cuts[chunk[2]]
                at = (chunk[1] * 2 + chunk[0]) * self.m + start
                which = (t * 2 + h) * self.m + i - at
                place = jnp.where((which >= 0) & (which < size), self.turn(order, chunk) + which, place)
            found.append(place)
        return found

    def phase(self, t):
        p = 0
        while t >= self.n - (self.n >> (p + 1)):
            p += 1
        return p


def fill_tables(plan, per_dev, kernels, owner, strip, strips, inter, index, psf_index, table, tell):
    e, width = plan.exposures, inter.shape[0]
    where = inter[...]
    match = where // (strips * per_dev) == owner
    place = (where // per_dev % strips - strip + 1) * per_dev + where % per_dev

    def pick(values):
        return jnp.sum(jnp.where(match, values, 0), axis=0, keepdims=True)

    live = pick(jnp.ones_like(where)) > 0
    slot = jnp.where(live, jnp.clip(pick(place), 0, 3 * per_dev - 1), -1)
    kernel_of = index[...]
    table[pl.ds(ROW, 1), :] = jnp.where(live, pick(kernel_of[:width]), kernels)
    table[pl.ds(COL, 1), :] = pick(kernel_of[width:])
    table[pl.ds(PSF, 1), :] = psf_index[...]

    down = lax.broadcasted_iota(jnp.int32, (e, e), 0)
    along = lax.broadcasted_iota(jnp.int32, (e, e), 1)
    first_along, last_along = plan.turns(owner, along[:1])

    def upright(line):
        return jnp.sum(jnp.where(down == along, line, 0), axis=1, keepdims=True)

    def flat(column):
        return jnp.sum(jnp.where(down == along, column, 0), axis=0, keepdims=True)

    slot_down, last_down = upright(slot), upright(last_along)
    before = (slot_down == slot) & (last_down < last_along)
    table[pl.ds(PREV, 1), :] = jnp.max(jnp.where(before, last_down + 1, 0), axis=0, keepdims=True)

    ready = jnp.where(live, slot, per_dev)
    for side, last_row in ((0, LAST_LOW), (1, LAST_OWN), (2, LAST_HIGH)):
        near = slot - side * per_dev
        near = jnp.where((near >= 0) & (near < per_dev) & live, near, -1)
        hit = near == down
        last = jnp.max(jnp.where(hit, last_along + 1, 0), axis=1, keepdims=True)
        if side == 1:
            table[pl.ds(last_row, 1), :] = flat(last)
            continue
        line = down[:, :1]
        first = jnp.min(jnp.where(hit, first_along, e + down), axis=1, keepdims=True)
        rank = jnp.sum(jnp.where(flat(first) < first, 1, 0), axis=1, keepdims=True)
        give = jnp.sum(jnp.where(rank == along, down, 0), axis=0, keepdims=True)
        arrival = jnp.sum(jnp.where(hit, rank, 0), axis=0, keepdims=True)
        ready = jnp.where(near >= 0, side * per_dev + arrival, ready)
        order = jnp.where(line < per_dev, last, e + 1) * e + line
        order_along = flat(order)
        done = jnp.sum(jnp.where(order_along < order, 1, 0), axis=1, keepdims=True)
        table[pl.ds(last_row, 1), :] = jnp.sum(jnp.where(done == along, last, 0), axis=0, keepdims=True)
        up = side // 2
        tell[up, pl.ds(GIVE, 1), :] = jnp.clip(give, 0, per_dev - 1)
        tell[up, pl.ds(RANK, 1), :] = jnp.clip(flat(done), 0, per_dev - 1)
    table[pl.ds(READY, 1), :] = ready


def gradient_kernel(
    plan, per_dev, inter, index, psf_index, scene, observed, weights, bank_h, psf_h, out,
    inter_v, index_v, psf_v, table_v, tell_v, table, tell, told, ready, stage, came, bank, bank_t, psf, psf_t, obs, ivar, terms, got,
    adj, run, leave, back, load_sem, tell_send, tell_recv, z_send, z_recv, rs_send, rs_recv, ag_send,
    ag_recv, back_send, back_recv,
):
    n, m = plan.n, plan.m
    e = plan.exposures
    kernels = bank_h.shape[0]
    owner = lax.axis_index("scene")
    strip = lax.axis_index("expo")
    strips = lax.axis_size("expo")
    ahead, behind = cut(per_dev, EDGE, CHUNK), cut(per_dev, CHUNK, EDGE)
    has = {0: strip > 0, 1: strip < strips - 1}

    barrier = pltpu.get_barrier_semaphore()
    for p in range(plan.bits):
        pl.semaphore_signal(
            barrier, inc=1, device_id={"scene": plan.partner(owner, 0, p)}, device_id_type=MESH
        )
    for up in range(2):

        @pl.when(has[up])
        def _(up=up):
            pl.semaphore_signal(
                barrier, inc=1, device_id={"expo": strip + 2 * up - 1}, device_id_type=MESH
            )

    given = [
        pltpu.make_async_copy(source, target, load_sem.at[9 + i])
        for i, (source, target) in enumerate(((inter, inter_v), (index, index_v), (psf_index, psf_v)))
    ]
    for load in given:
        load.start()
    loads = [
        pltpu.make_async_copy(scene, ready.at[pl.ds(per_dev, per_dev)], load_sem.at[0]),
        pltpu.make_async_copy(bank_h, bank.at[pl.ds(0, kernels)], load_sem.at[1]),
        pltpu.make_async_copy(psf_h, psf, load_sem.at[2]),
    ]
    for h in range(2):
        home = plan.unit(owner, h, n - 1)
        for source, target in ((observed, obs), (weights, ivar)):
            loads.append(
                pltpu.make_async_copy(
                    source.at[pl.ds(home, m)], target.at[pl.ds(h * m, m)], load_sem.at[len(loads)]
                )
            )
    for load in loads:
        load.start()

    for load in given:
        load.wait()
    fill_tables(
        plan, per_dev, kernels, owner, strip, strips, inter_v, index_v, psf_v, table_v, tell_v
    )
    own_table = pltpu.make_async_copy(table_v, table, load_sem.at[7])
    own_tell = pltpu.make_async_copy(tell_v, tell, load_sem.at[8])
    own_tell.start()
    own_table.start()
    own_tell.wait()
    pl.semaphore_wait(
        barrier, plan.bits + jnp.where(has[0], 1, 0) + jnp.where(has[1], 1, 0)
    )

    def tell_copy(up):
        return pltpu.make_async_remote_copy(
            src_ref=tell.at[up],
            dst_ref=told.at[1 - up],
            send_sem=tell_send.at[up],
            recv_sem=tell_recv.at[1 - up],
            device_id={"expo": strip + 2 * up - 1},
            device_id_type=MESH,
        )

    for up in range(2):

        @pl.when(has[up])
        def _(up=up):
            tell_copy(up).start()

    bank[kernels] = jnp.zeros(bank.shape[1:], bank.dtype)
    bank_t[kernels] = jnp.zeros(bank.shape[1:], bank.dtype)
    run[0] = jnp.zeros(run.shape[1:], run.dtype)
    loads[0].wait()
    for up in range(2):

        @pl.when(jnp.logical_not(has[up]))
        def _(up=up):
            def wipe(i, carry):
                told[up, RANK, i] = 0
                back[up * per_dev + i] = jnp.zeros(back.shape[1:], back.dtype)
                return carry

            lax.fori_loop(0, per_dev, wipe, 0)

        @pl.when(has[up])
        def _(up=up):
            tell_copy(1 - up).wait_recv()

    def z_copy(up, q):
        start, size = ahead[q]
        return pltpu.make_async_remote_copy(
            src_ref=stage.at[pl.ds(up * per_dev + start, size)],
            dst_ref=came.at[pl.ds(up * per_dev + start, size)],
            send_sem=z_send.at[up * len(ahead) + q],
            recv_sem=z_recv.at[up * len(ahead) + q],
            device_id={"expo": strip + 2 * up - 1},
            device_id_type=MESH,
        )

    for q, (start, size) in enumerate(ahead):
        for up in range(2):

            @pl.when(has[up])
            def _(up=up, q=q, start=start, size=size):
                for i in range(start, start + size):
                    stage[up * per_dev + i] = ready[per_dev + told[up, GIVE, i]]
                z_copy(up, q).start()

    for load in loads[1:]:
        load.wait()

    turn_steps = sum(t < n // 2 for _, t, _ in plan.made)

    def turn_some(step):
        for source, target, count in ((bank, bank_t, kernels), (psf, psf_t, psf.shape[0])):

            def turn(i, carry, source=source, target=target):
                target[i] = source[i].T
                return carry

            lax.fori_loop(step * count // turn_steps, (step + 1) * count // turn_steps, turn, 0)

    own_table.wait()
    taken = [0]

    def take(turns):
        while taken[0] < len(ahead) and ahead[taken[0]][0] < turns:
            q = taken[0]
            taken[0] += 1
            for up in range(2):

                @pl.when(has[1 - up])
                def _(up=up, q=q):
                    z_copy(up, q).wait_recv()
                    for i in range(ahead[q][0], sum(ahead[q])):
                        ready[(1 - up) * 2 * per_dev + i] = came[up * per_dev + i]

    def spot(h, t, k):
        return plan.base(h, t) + plan.cuts[k][0], plan.cuts[k][1]

    def slot(h, t, k):
        return (h * n + t) * plan.chunks + k

    def scatter_copy(h, t, k):
        return pltpu.make_async_remote_copy(
            src_ref=terms.at[pl.ds(*spot(h, t, k))],
            dst_ref=got.at[pl.ds(*spot(h, t, k))],
            send_sem=rs_send.at[slot(h, t, k)],
            recv_sem=rs_recv.at[slot(h, t, k)],
            device_id={"scene": plan.partner(owner, h, plan.phase(t))},
            device_id_type=MESH,
        )

    def gather_copy(h, t, p, k):
        target = t - (n >> (p + 1))
        return pltpu.make_async_remote_copy(
            src_ref=adj.at[pl.ds(*spot(h, t, k))],
            dst_ref=adj.at[pl.ds(*spot(h, target, k))],
            send_sem=ag_send.at[slot(h, target, k)],
            recv_sem=ag_recv.at[slot(h, target, k)],
            device_id={"scene": plan.partner(owner, h, p)},
            device_id_type=MESH,
        )

    def make_terms(h, t, k):
        where, size = spot(h, t, k)
        first = plan.unit(owner, h, t) + plan.cuts[k][0]
        inner = [
            dot(ready[table[READY, first + a]], bank[table[COL, first + a]], NT).astype(jnp.bfloat16)
            for a in range(size)
        ]
        term = [
            dot(bank[table[ROW, first + a]], x, NN).astype(jnp.bfloat16) for a, x in enumerate(inner)
        ]
        for a, x in enumerate(term):
            terms[where + a] = x

    def arrived(t):
        return [t - (n >> (q + 1)) for q in range(plan.bits) if t >= n - (n >> (q + 1))]

    def summed(h, t, k, i):
        total = terms[spot(h, t, k)[0] + i].astype(jnp.float32)
        for source in arrived(t):
            total = total + got[spot(h, source, k)[0] + i].astype(jnp.float32)
        return total.astype(jnp.bfloat16)

    def pass_on(h, t, k):
        where, size = spot(h, t, k)
        for i in range(size):
            terms[where + i] = summed(h, t, k, i)

    def psf_pass(h, k):
        where, size = spot(h, n - 1, k)
        start = plan.cuts[k][0]
        first = plan.unit(owner, h, n - 1) + start
        which = [table[PSF, first + a] for a in range(size)]
        half = [dot(summed(h, n - 1, k, a), psf[q], NT).astype(jnp.bfloat16) for a, q in enumerate(which)]
        model = [dot(psf[q], x, NN) for q, x in zip(which, half)]
        weighted = []
        for a, x in enumerate(model):
            here = h * m + start + a
            x = ivar[here].astype(jnp.float32) * (x - obs[here].astype(jnp.float32))
            weighted.append(x.astype(jnp.bfloat16))
        half = [dot(x, psf[q], NN).astype(jnp.bfloat16) for q, x in zip(which, weighted)]
        for a, (q, x) in enumerate(zip(which, half)):
            adj[where + a] = dot(psf_t[q], x, NN).astype(jnp.bfloat16)

    for t in range(n):
        for k in range(plan.chunks):
            for h in range(2):
                take(plan.turn(plan.made, (h, t, k)) + plan.cuts[k][1])
                make_terms(h, t, k)
                for source in arrived(t):
                    scatter_copy(h, source, k).wait_recv()
                if t < n // 2:
                    scatter_copy(h, t, k).start()
                    turn_some(plan.made.index((h, t, k)))
                elif t < n - 1:
                    pass_on(h, t, k)
                    scatter_copy(h, t, k).start()
                else:
                    psf_pass(h, k)
                    for p in reversed(range(plan.bits)):
                        gather_copy(h, n - 1, p, k).start()

    for up in range(2):

        @pl.when(has[up])
        def _(up=up):
            tell_copy(up).wait_send()
            for q in range(len(ahead)):
                z_copy(up, q).wait_send()

    def back_copy(up, q):
        start, size = behind[q]
        return pltpu.make_async_remote_copy(
            src_ref=leave.at[pl.ds(up * per_dev + start, size)],
            dst_ref=back.at[pl.ds((1 - up) * per_dev + start, size)],
            send_sem=back_send.at[up * len(behind) + q],
            recv_sem=back_recv.at[(1 - up) * len(behind) + q],
            device_id={"expo": strip + 2 * up - 1},
            device_id_type=MESH,
        )

    def pull(h, t, k):
        where, size = spot(h, t, k)
        first = plan.unit(owner, h, t) + plan.cuts[k][0]
        turn = plan.turn(plan.pulled, (h, t, k))
        spread = [
            dot(adj[where + a], bank[table[COL, first + a]], NN).astype(jnp.bfloat16) for a in range(size)
        ]
        pulled = [dot(bank_t[table[ROW, first + a]], x, NN) for a, x in enumerate(spread)]
        for a, x in enumerate(pulled):
            run[1 + turn + a] = x + run[table[PREV, first + a]]

        for q, (start, count) in enumerate(behind):
            if turn < max(1, e - per_dev + start + count) <= turn + size:
                for up, last in ((0, LAST_LOW), (1, LAST_HIGH)):

                    @pl.when(has[up])
                    def _(up=up, last=last, q=q, start=start, count=count):
                        for a in range(start, start + count):
                            leave[up * per_dev + a] = run[table[last, a]].astype(leave.dtype)
                        back_copy(up, q).start()

    for h, t, k in plan.pulled:
        if t < n - 1:
            last = plan.phase(t)
            gather_copy(h, t + (n >> (last + 1)), last, k).wait_recv()
            for p in reversed(range(last)):
                gather_copy(h, t, p, k).start()
        pull(h, t, k)

    for t in range(n - 1):
        for k in range(plan.chunks):
            for h in range(2):
                scatter_copy(h, t, k).wait_send()
                p = plan.phase(t)
                gather_copy(h, t + (n >> (p + 1)), p, k).wait_send()

    for up in range(2):

        @pl.when(has[up])
        def _(up=up):
            for q in range(len(behind)):
                back_copy(1 - up, q).wait_recv()

    def own(b, carry):
        low = back[told[0, RANK, b]].astype(jnp.float32)
        high = back[per_dev + told[1, RANK, b]].astype(jnp.float32)
        out[b] = run[table[LAST_OWN, b]] + (low + high)
        return carry

    lax.fori_loop(0, per_dev, own, 0, unroll=4)

    for up in range(2):

        @pl.when(has[up])
        def _(up=up):
            for q in range(len(behind)):
                back_copy(up, q).wait_send()


def on_device(
    scene,
    observed,
    inverse_variance,
    intersection,
    resample_index,
    psf_index,
    resample_bank,
    psf_bank,
):
    per_dev, side = scene.shape[0], scene.shape[1:]
    e = intersection.shape[0]
    plan = Plan(lax.axis_size("scene"), e)
    slots = 2 * plan.n * plan.chunks
    pieces = len(cut(per_dev, EDGE, EDGE)) + 1
    kernels, psfs = resample_bank.shape[0], psf_bank.shape[0]
    dtype = scene.dtype
    hbm = pl.BlockSpec(memory_space=pl.ANY)
    dma = pltpu.SemaphoreType.DMA
    blocks = lambda count, kind=dtype: pltpu.VMEM((count, *side), kind)
    return pl.pallas_call(
        functools.partial(gradient_kernel, plan, per_dev),
        out_shape=pltpu.VMEM((per_dev, *side), jnp.float32),
        in_specs=[hbm] * 8,
        out_specs=pl.BlockSpec(memory_space=pltpu.VMEM),
        scratch_shapes=[
            pltpu.VMEM((intersection.shape[1], e), jnp.int32),
            pltpu.VMEM((resample_index.shape[1], e), jnp.int32),
            pltpu.VMEM((1, e), jnp.int32),
            pltpu.VMEM((8, e), jnp.int32),
            pltpu.VMEM((2, 2, e), jnp.int32),
            pltpu.SMEM((8, e), jnp.int32),
            pltpu.SMEM((2, 2, e), jnp.int32),
            pltpu.SMEM((2, 2, e), jnp.int32),
            blocks(3 * per_dev),
            blocks(2 * per_dev),
            blocks(2 * per_dev),
            blocks(kernels + 1),
            blocks(kernels + 1),
            blocks(psfs),
            blocks(psfs),
            blocks(2 * plan.m),
            blocks(2 * plan.m),
            blocks(e),
            blocks(e),
            blocks(e),
            blocks(e + 1, jnp.float32),
            blocks(2 * per_dev),
            blocks(2 * per_dev),
            dma((12,)),
            dma((2,)),
            dma((2,)),
            dma((2 * pieces,)),
            dma((2 * pieces,)),
            dma((slots,)),
            dma((slots,)),
            dma((slots,)),
            dma((slots,)),
            dma((2 * pieces,)),
            dma((2 * pieces,)),
        ],
        compiler_params=pltpu.CompilerParams(
            collective_id=0, has_side_effects=True, vmem_limit_bytes=VMEM_LIMIT
        ),
        name="gradient",
    )(
        intersection.T, resample_index.T, psf_index.reshape(1, e), scene, observed, inverse_variance,
        resample_bank, psf_bank,
    )


def solution(mesh):
    return jax.shard_map(
        on_device,
        mesh=mesh,
        in_specs=(
            P(("scene", "expo"), None, None),
            P("expo", None, None),
            P("expo", None, None),
            P("expo", None),
            P("expo", None),
            P("expo"),
            P(),
            P(),
        ),
        out_specs=P(("scene", "expo"), None, None),
        check_vma=False,
    )
```

```python
import functools

import jax
import jax.numpy as jnp
from jax import lax
from jax.experimental import pallas as pl
from jax.experimental.pallas import tpu as pltpu
from jax.sharding import PartitionSpec as P

MESH = pl.DeviceIdType.MESH
CHUNK = 4
EDGE = 2
VMEM_LIMIT = 54 * 1024 * 1024

READY, ROW, COL, PREV, PSF, LAST_LOW, LAST_HIGH, LAST_OWN = range(8)
GIVE, RANK = range(2)


def dot(a, b, dims):
    return lax.dot_general(a, b, (dims, ((), ())), preferred_element_type=jnp.float32)


NN = ((1,), (0,))
NT = ((1,), (1,))


def cut(length, first, last):
    sizes = [min(first, length)]
    while sum(sizes) < length:
        rest = length - sum(sizes)
        sizes.append(min(CHUNK, rest - last) if rest > last else rest)
    return [(sum(sizes[:i]), size) for i, size in enumerate(sizes)]


class Plan:
    def __init__(self, owners, exposures):
        self.n = owners
        self.bits = owners.bit_length() - 1
        assert 1 << self.bits == owners
        self.exposures = exposures
        self.half = exposures // 2
        self.m = self.half // owners
        self.cuts = cut(self.m, EDGE, EDGE)
        self.chunks = len(self.cuts)
        self.made, self.pulled = [], []
        for t in range(self.n):
            self.made += [(h, t, k) for k in range(self.chunks) for h in range(2)]
        for hops in range(self.bits + 1):
            units = [t for t in reversed(range(self.n)) if self.hops(t) == hops]
            self.pulled += [(h, t, k) for k in range(self.chunks) for t in units for h in range(2)]

    def bit(self, h, p):
        return p if h == 0 else self.bits - 1 - p

    def value(self, owner, h, p):
        return (owner // (1 << self.bit(h, p))) % 2

    def partner(self, owner, h, p):
        step = 1 << self.bit(h, p)
        return owner + step - 2 * step * self.value(owner, h, p)

    def unit(self, owner, h, t):
        u = 0
        for p in range(self.bits):
            weight = self.n >> (p + 1)
            v = self.value(owner, h, p)
            u = u + weight * (v if t & weight else 1 - v)
        return h * self.half + u * self.m

    def base(self, h, t):
        return h * self.half + t * self.m

    def hops(self, t):
        return 0 if t == self.n - 1 else 1 + self.hops(t + (self.n >> (self.phase(t) + 1)))

    def turn(self, order, chunk):
        return sum(self.cuts[k][1] for _, _, k in order[: order.index(chunk)])

    def turns(self, owner, j):
        h, u, i = j // self.half, j % self.half // self.m, j % self.m
        me = [(self.unit(owner, h, self.n - 1) - h * self.half) // self.m for h in range(2)]
        t = self.n - 1 - jnp.bitwise_xor(u, jnp.where(h == 0, me[0], me[1]))
        found = []
        for order in (self.made, self.pulled):
            place = jnp.zeros_like(j)
            for chunk in order:
                start, size = self.cuts[chunk[2]]
                at = (chunk[1] * 2 + chunk[0]) * self.m + start
                which = (t * 2 + h) * self.m + i - at
                place = jnp.where((which >= 0) & (which < size), self.turn(order, chunk) + which, place)
            found.append(place)
        return found

    def phase(self, t):
        p = 0
        while t >= self.n - (self.n >> (p + 1)):
            p += 1
        return p


def fill_tables(plan, per_dev, kernels, owner, strip, strips, inter, index, psf_index, table, tell):
    e, width = plan.exposures, inter.shape[0]
    where = inter[...]
    match = where // (strips * per_dev) == owner
    place = (where // per_dev % strips - strip + 1) * per_dev + where % per_dev

    def pick(values):
        return jnp.sum(jnp.where(match, values, 0), axis=0, keepdims=True)

    live = pick(jnp.ones_like(where)) > 0
    slot = jnp.where(live, jnp.clip(pick(place), 0, 3 * per_dev - 1), -1)
    kernel_of = index[...]
    table[pl.ds(ROW, 1), :] = jnp.where(live, pick(kernel_of[:width]), kernels)
    table[pl.ds(COL, 1), :] = pick(kernel_of[width:])
    table[pl.ds(PSF, 1), :] = psf_index[...]

    down = lax.broadcasted_iota(jnp.int32, (e, e), 0)
    along = lax.broadcasted_iota(jnp.int32, (e, e), 1)
    first_along, last_along = plan.turns(owner, along[:1])

    def upright(line):
        return jnp.sum(jnp.where(down == along, line, 0), axis=1, keepdims=True)

    def flat(column):
        return jnp.sum(jnp.where(down == along, column, 0), axis=0, keepdims=True)

    slot_down, last_down = upright(slot), upright(last_along)
    before = (slot_down == slot) & (last_down < last_along)
    table[pl.ds(PREV, 1), :] = jnp.max(jnp.where(before, last_down + 1, 0), axis=0, keepdims=True)

    ready = jnp.where(live, slot, per_dev)
    for side, last_row in ((0, LAST_LOW), (1, LAST_OWN), (2, LAST_HIGH)):
        near = slot - side * per_dev
        near = jnp.where((near >= 0) & (near < per_dev) & live, near, -1)
        hit = near == down
        last = jnp.max(jnp.where(hit, last_along + 1, 0), axis=1, keepdims=True)
        if side == 1:
            table[pl.ds(last_row, 1), :] = flat(last)
            continue
        line = down[:, :1]
        first = jnp.min(jnp.where(hit, first_along, e + down), axis=1, keepdims=True)
        rank = jnp.sum(jnp.where(flat(first) < first, 1, 0), axis=1, keepdims=True)
        give = jnp.sum(jnp.where(rank == along, down, 0), axis=0, keepdims=True)
        arrival = jnp.sum(jnp.where(hit, rank, 0), axis=0, keepdims=True)
        ready = jnp.where(near >= 0, side * per_dev + arrival, ready)
        order = jnp.where(line < per_dev, last, e + 1) * e + line
        order_along = flat(order)
        done = jnp.sum(jnp.where(order_along < order, 1, 0), axis=1, keepdims=True)
        table[pl.ds(last_row, 1), :] = jnp.sum(jnp.where(done == along, last, 0), axis=0, keepdims=True)
        up = side // 2
        tell[up, pl.ds(GIVE, 1), :] = jnp.clip(give, 0, per_dev - 1)
        tell[up, pl.ds(RANK, 1), :] = jnp.clip(flat(done), 0, per_dev - 1)
    table[pl.ds(READY, 1), :] = ready


def gradient_kernel(
    plan, per_dev, inter, index, psf_index, scene, observed, weights, bank_h, psf_h, out, above,
    inter_v, index_v, psf_v, table_v, tell_v, table, tell, told, ready, stage, came, bank, bank_t, psf, psf_t, obs, ivar, terms, got,
    adj, run, leave, back, load_sem, tell_send, tell_recv, z_send, z_recv, rs_send, rs_recv, ag_send,
    ag_recv, back_send, back_recv,
):
    n, m = plan.n, plan.m
    e = plan.exposures
    kernels = bank_h.shape[0]
    owner = lax.axis_index("scene")
    strip = lax.axis_index("expo")
    strips = lax.axis_size("expo")
    ahead, behind = cut(per_dev, EDGE, CHUNK), cut(per_dev, CHUNK, EDGE)
    has = {0: strip > 0, 1: strip < strips - 1}

    barrier = pltpu.get_barrier_semaphore()
    for p in range(plan.bits):
        pl.semaphore_signal(
            barrier, inc=1, device_id={"scene": plan.partner(owner, 0, p)}, device_id_type=MESH
        )
    for up in range(2):

        @pl.when(has[up])
        def _(up=up):
            pl.semaphore_signal(
                barrier, inc=1, device_id={"expo": strip + 2 * up - 1}, device_id_type=MESH
            )

    given = [
        pltpu.make_async_copy(source, target, load_sem.at[9 + i])
        for i, (source, target) in enumerate(((inter, inter_v), (index, index_v), (psf_index, psf_v)))
    ]
    for load in given:
        load.start()
    loads = [
        pltpu.make_async_copy(scene, ready.at[pl.ds(per_dev, per_dev)], load_sem.at[0]),
        pltpu.make_async_copy(bank_h, bank.at[pl.ds(0, kernels)], load_sem.at[1]),
        pltpu.make_async_copy(psf_h, psf, load_sem.at[2]),
    ]
    for h in range(2):
        home = plan.unit(owner, h, n - 1)
        for source, target in ((observed, obs), (weights, ivar)):
            loads.append(
                pltpu.make_async_copy(
                    source.at[pl.ds(home, m)], target.at[pl.ds(h * m, m)], load_sem.at[len(loads)]
                )
            )
    for load in loads:
        load.start()

    for load in given:
        load.wait()
    fill_tables(
        plan, per_dev, kernels, owner, strip, strips, inter_v, index_v, psf_v, table_v, tell_v
    )
    own_table = pltpu.make_async_copy(table_v, table, load_sem.at[7])
    own_tell = pltpu.make_async_copy(tell_v, tell, load_sem.at[8])
    own_tell.start()
    own_table.start()
    own_tell.wait()
    pl.semaphore_wait(
        barrier, plan.bits + jnp.where(has[0], 1, 0) + jnp.where(has[1], 1, 0)
    )

    def tell_copy(up):
        return pltpu.make_async_remote_copy(
            src_ref=tell.at[up],
            dst_ref=told.at[1 - up],
            send_sem=tell_send.at[up],
            recv_sem=tell_recv.at[1 - up],
            device_id={"expo": strip + 2 * up - 1},
            device_id_type=MESH,
        )

    for up in range(2):

        @pl.when(has[up])
        def _(up=up):
            tell_copy(up).start()

    bank[kernels] = jnp.zeros(bank.shape[1:], bank.dtype)
    bank_t[kernels] = jnp.zeros(bank.shape[1:], bank.dtype)
    run[0] = jnp.zeros(run.shape[1:], run.dtype)
    loads[0].wait()
    for up in range(2):

        @pl.when(jnp.logical_not(has[up]))
        def _(up=up):
            def wipe(i, carry):
                told[up, RANK, i] = 0
                back[up * per_dev + i] = jnp.zeros(back.shape[1:], back.dtype)
                return carry

            lax.fori_loop(0, per_dev, wipe, 0)

        @pl.when(has[up])
        def _(up=up):
            tell_copy(1 - up).wait_recv()

    def z_copy(up, q):
        start, size = ahead[q]
        return pltpu.make_async_remote_copy(
            src_ref=stage.at[pl.ds(up * per_dev + start, size)],
            dst_ref=came.at[pl.ds(up * per_dev + start, size)],
            send_sem=z_send.at[up * len(ahead) + q],
            recv_sem=z_recv.at[up * len(ahead) + q],
            device_id={"expo": strip + 2 * up - 1},
            device_id_type=MESH,
        )

    for q, (start, size) in enumerate(ahead):
        for up in range(2):

            @pl.when(has[up])
            def _(up=up, q=q, start=start, size=size):
                for i in range(start, start + size):
                    stage[up * per_dev + i] = ready[per_dev + told[up, GIVE, i]]
                z_copy(up, q).start()

    for load in loads[1:]:
        load.wait()

    turn_steps = sum(t < n // 2 for _, t, _ in plan.made)

    def turn_some(step):
        for source, target, count in ((bank, bank_t, kernels), (psf, psf_t, psf.shape[0])):

            def turn(i, carry, source=source, target=target):
                target[i] = source[i].T
                return carry

            lax.fori_loop(step * count // turn_steps, (step + 1) * count // turn_steps, turn, 0)

    own_table.wait()
    taken = [0]

    def take(turns):
        while taken[0] < len(ahead) and ahead[taken[0]][0] < turns:
            q = taken[0]
            taken[0] += 1
            for up in range(2):

                @pl.when(has[1 - up])
                def _(up=up, q=q):
                    z_copy(up, q).wait_recv()
                    for i in range(ahead[q][0], sum(ahead[q])):
                        ready[(1 - up) * 2 * per_dev + i] = came[up * per_dev + i]

    def spot(h, t, k):
        return plan.base(h, t) + plan.cuts[k][0], plan.cuts[k][1]

    def slot(h, t, k):
        return (h * n + t) * plan.chunks + k

    def scatter_copy(h, t, k):
        return pltpu.make_async_remote_copy(
            src_ref=terms.at[pl.ds(*spot(h, t, k))],
            dst_ref=got.at[pl.ds(*spot(h, t, k))],
            send_sem=rs_send.at[slot(h, t, k)],
            recv_sem=rs_recv.at[slot(h, t, k)],
            device_id={"scene": plan.partner(owner, h, plan.phase(t))},
            device_id_type=MESH,
        )

    def gather_copy(h, t, p, k):
        target = t - (n >> (p + 1))
        return pltpu.make_async_remote_copy(
            src_ref=adj.at[pl.ds(*spot(h, t, k))],
            dst_ref=adj.at[pl.ds(*spot(h, target, k))],
            send_sem=ag_send.at[slot(h, target, k)],
            recv_sem=ag_recv.at[slot(h, target, k)],
            device_id={"scene": plan.partner(owner, h, p)},
            device_id_type=MESH,
        )

    def make_terms(h, t, k):
        where, size = spot(h, t, k)
        first = plan.unit(owner, h, t) + plan.cuts[k][0]
        inner = [
            dot(ready[table[READY, first + a]], bank[table[COL, first + a]], NT).astype(jnp.bfloat16)
            for a in range(size)
        ]
        term = [
            dot(bank[table[ROW, first + a]], x, NN).astype(jnp.bfloat16) for a, x in enumerate(inner)
        ]
        for a, x in enumerate(term):
            terms[where + a] = x

    def arrived(t):
        return [t - (n >> (q + 1)) for q in range(plan.bits) if t >= n - (n >> (q + 1))]

    def summed(h, t, k, i):
        total = terms[spot(h, t, k)[0] + i].astype(jnp.float32)
        for source in arrived(t):
            total = total + got[spot(h, source, k)[0] + i].astype(jnp.float32)
        return total.astype(jnp.bfloat16)

    def pass_on(h, t, k):
        where, size = spot(h, t, k)
        for i in range(size):
            terms[where + i] = summed(h, t, k, i)

    def psf_pass(h, k):
        where, size = spot(h, n - 1, k)
        start = plan.cuts[k][0]
        first = plan.unit(owner, h, n - 1) + start
        which = [table[PSF, first + a] for a in range(size)]
        half = [dot(summed(h, n - 1, k, a), psf[q], NT).astype(jnp.bfloat16) for a, q in enumerate(which)]
        model = [dot(psf[q], x, NN) for q, x in zip(which, half)]
        weighted = []
        for a, x in enumerate(model):
            here = h * m + start + a
            x = ivar[here].astype(jnp.float32) * (x - obs[here].astype(jnp.float32))
            weighted.append(x.astype(jnp.bfloat16))
        half = [dot(x, psf[q], NN).astype(jnp.bfloat16) for q, x in zip(which, weighted)]
        for a, (q, x) in enumerate(zip(which, half)):
            adj[where + a] = dot(psf_t[q], x, NN).astype(jnp.bfloat16)

    for t in range(n):
        for k in range(plan.chunks):
            for h in range(2):
                take(plan.turn(plan.made, (h, t, k)) + plan.cuts[k][1])
                make_terms(h, t, k)
                for source in arrived(t):
                    scatter_copy(h, source, k).wait_recv()
                if t < n // 2:
                    scatter_copy(h, t, k).start()
                    turn_some(plan.made.index((h, t, k)))
                elif t < n - 1:
                    pass_on(h, t, k)
                    scatter_copy(h, t, k).start()
                else:
                    psf_pass(h, k)
                    for p in reversed(range(plan.bits)):
                        gather_copy(h, n - 1, p, k).start()

    for up in range(2):

        @pl.when(has[up])
        def _(up=up):
            tell_copy(up).wait_send()
            for q in range(len(ahead)):
                z_copy(up, q).wait_send()

    def back_copy(up, q):
        start, size = behind[q]
        return pltpu.make_async_remote_copy(
            src_ref=leave.at[pl.ds(up * per_dev + start, size)],
            dst_ref=back.at[pl.ds((1 - up) * per_dev + start, size)],
            send_sem=back_send.at[up * len(behind) + q],
            recv_sem=back_recv.at[(1 - up) * len(behind) + q],
            device_id={"expo": strip + 2 * up - 1},
            device_id_type=MESH,
        )

    def pull(h, t, k):
        where, size = spot(h, t, k)
        first = plan.unit(owner, h, t) + plan.cuts[k][0]
        turn = plan.turn(plan.pulled, (h, t, k))
        spread = [
            dot(adj[where + a], bank[table[COL, first + a]], NN).astype(jnp.bfloat16) for a in range(size)
        ]
        pulled = [dot(bank_t[table[ROW, first + a]], x, NN) for a, x in enumerate(spread)]
        for a, x in enumerate(pulled):
            run[1 + turn + a] = x + run[table[PREV, first + a]]

        for q, (start, count) in enumerate(behind):
            if turn < max(1, e - per_dev + start + count) <= turn + size:
                for up, last in ((0, LAST_LOW), (1, LAST_HIGH)):

                    @pl.when(has[up])
                    def _(up=up, last=last, q=q, start=start, count=count):
                        for a in range(start, start + count):
                            leave[up * per_dev + a] = run[table[last, a]].astype(leave.dtype)
                        back_copy(up, q).start()

    for h, t, k in plan.pulled:
        if t < n - 1:
            last = plan.phase(t)
            gather_copy(h, t + (n >> (last + 1)), last, k).wait_recv()
            for p in reversed(range(last)):
                gather_copy(h, t, p, k).start()
        pull(h, t, k)

    for t in range(n - 1):
        for k in range(plan.chunks):
            for h in range(2):
                scatter_copy(h, t, k).wait_send()
                p = plan.phase(t)
                gather_copy(h, t + (n >> (p + 1)), p, k).wait_send()

    for up in range(2):

        @pl.when(has[up])
        def _(up=up):
            for q in range(len(behind)):
                back_copy(1 - up, q).wait_recv()

    def own(b, carry):
        out[b] = run[table[LAST_OWN, b]] + back[told[0, RANK, b]].astype(jnp.float32)
        above[b] = back[per_dev + told[1, RANK, b]]
        return carry

    lax.fori_loop(0, per_dev, own, 0, unroll=4)

    for up in range(2):

        @pl.when(has[up])
        def _(up=up):
            for q in range(len(behind)):
                back_copy(up, q).wait_send()


def on_device(
    scene,
    observed,
    inverse_variance,
    intersection,
    resample_index,
    psf_index,
    resample_bank,
    psf_bank,
):
    per_dev, side = scene.shape[0], scene.shape[1:]
    e = intersection.shape[0]
    plan = Plan(lax.axis_size("scene"), e)
    slots = 2 * plan.n * plan.chunks
    pieces = len(cut(per_dev, EDGE, EDGE)) + 1
    kernels, psfs = resample_bank.shape[0], psf_bank.shape[0]
    dtype = scene.dtype
    hbm = pl.BlockSpec(memory_space=pl.ANY)
    dma = pltpu.SemaphoreType.DMA
    blocks = lambda count, kind=dtype: pltpu.VMEM((count, *side), kind)
    grad, above = pl.pallas_call(
        functools.partial(gradient_kernel, plan, per_dev),
        out_shape=[blocks(per_dev, jnp.float32), blocks(per_dev)],
        in_specs=[hbm] * 8,
        out_specs=[pl.BlockSpec(memory_space=pltpu.VMEM)] * 2,
        scratch_shapes=[
            pltpu.VMEM((intersection.shape[1], e), jnp.int32),
            pltpu.VMEM((resample_index.shape[1], e), jnp.int32),
            pltpu.VMEM((1, e), jnp.int32),
            pltpu.VMEM((8, e), jnp.int32),
            pltpu.VMEM((2, 2, e), jnp.int32),
            pltpu.SMEM((8, e), jnp.int32),
            pltpu.SMEM((2, 2, e), jnp.int32),
            pltpu.SMEM((2, 2, e), jnp.int32),
            blocks(3 * per_dev),
            blocks(2 * per_dev),
            blocks(2 * per_dev),
            blocks(kernels + 1),
            blocks(kernels + 1),
            blocks(psfs),
            blocks(psfs),
            blocks(2 * plan.m),
            blocks(2 * plan.m),
            blocks(e),
            blocks(e),
            blocks(e),
            blocks(e + 1, jnp.float32),
            blocks(2 * per_dev),
            blocks(2 * per_dev),
            dma((12,)),
            dma((2,)),
            dma((2,)),
            dma((2 * pieces,)),
            dma((2 * pieces,)),
            dma((slots,)),
            dma((slots,)),
            dma((slots,)),
            dma((slots,)),
            dma((2 * pieces,)),
            dma((2 * pieces,)),
        ],
        compiler_params=pltpu.CompilerParams(
            collective_id=0, has_side_effects=True, vmem_limit_bytes=VMEM_LIMIT
        ),
        name="gradient",
    )(
        intersection.T, resample_index.T, psf_index.reshape(1, e), scene, observed, inverse_variance,
        resample_bank, psf_bank,
    )
    return grad + above.astype(jnp.float32)


def solution(mesh):
    return jax.shard_map(
        on_device,
        mesh=mesh,
        in_specs=(
            P(("scene", "expo"), None, None),
            P("expo", None, None),
            P("expo", None, None),
            P("expo", None),
            P("expo", None),
            P("expo"),
            P(),
            P(),
        ),
        out_specs=P(("scene", "expo"), None, None),
        check_vma=False,
    )
```

```python
import functools

import jax
import jax.numpy as jnp
from jax import lax
from jax.experimental import pallas as pl
from jax.experimental.pallas import tpu as pltpu
from jax.sharding import PartitionSpec as P

MESH = pl.DeviceIdType.MESH
CHUNK = 4
EDGE = 2
VMEM_LIMIT = 56 * 1024 * 1024

READY, ROW, COL, PREV, PSF, LAST_LOW, LAST_HIGH, LAST_OWN = range(8)
GIVE, RANK = range(2)


def dot(a, b, dims):
    return lax.dot_general(a, b, (dims, ((), ())), preferred_element_type=jnp.float32)


NN = ((1,), (0,))
NT = ((1,), (1,))


def cut(length, first, last):
    sizes = [min(first, length)]
    while sum(sizes) < length:
        rest = length - sum(sizes)
        sizes.append(min(CHUNK, rest - last) if rest > last else rest)
    return [(sum(sizes[:i]), size) for i, size in enumerate(sizes)]


ORDER = (
    10, 0, 4, 11, 210, 110, 3, 113, 100, 104, 14, 310, 211, 12, 101, 13,
    1, 114, 200, 112, 510, 214, 2, 111, 204, 203, 103, 212, 102, 213, 201, 710,
    202, 300, 700, 304, 311, 303, 704, 312, 301, 314, 703, 711, 302, 500, 701, 313,
    611, 610, 702, 600, 713, 603, 714, 511, 712, 503, 604, 612, 504, 512, 501, 601,
    514, 614, 502, 602, 613, 513, 411, 403, 410, 404, 412, 401, 400, 414, 413, 402,
)


class Plan:
    def __init__(self, owners, exposures):
        self.n = owners
        self.bits = owners.bit_length() - 1
        assert 1 << self.bits == owners
        self.exposures = exposures
        self.half = exposures // 2
        self.m = self.half // owners
        self.cuts = cut(self.m, EDGE, EDGE)
        self.chunks = len(self.cuts)
        chunks = range(self.chunks)
        if (self.n, self.chunks) == (4, 5):
            self.steps = [(e // 400, e % 100 // 10, e % 400 // 100, e % 10) for e in ORDER]
        else:
            self.steps = [(0, h, t, k) for t in range(self.n) for k in chunks for h in range(2)]
            for hops in range(self.bits + 1):
                units = [t for t in reversed(range(self.n)) if self.hops(t) == hops]
                self.steps += [(1, h, t, k) for k in chunks for t in units for h in range(2)]
        self.made = [chunk for pulls, *chunk in self.steps if not pulls]
        self.pulled = [chunk for pulls, *chunk in self.steps if pulls]

    def bit(self, h, p):
        return p if h == 0 else self.bits - 1 - p

    def value(self, owner, h, p):
        return (owner // (1 << self.bit(h, p))) % 2

    def partner(self, owner, h, p):
        step = 1 << self.bit(h, p)
        return owner + step - 2 * step * self.value(owner, h, p)

    def unit(self, owner, h, t):
        u = 0
        for p in range(self.bits):
            weight = self.n >> (p + 1)
            v = self.value(owner, h, p)
            u = u + weight * (v if t & weight else 1 - v)
        return h * self.half + u * self.m

    def base(self, h, t):
        return h * self.half + t * self.m

    def hops(self, t):
        return 0 if t == self.n - 1 else 1 + self.hops(t + (self.n >> (self.phase(t) + 1)))

    def turn(self, order, chunk):
        return sum(self.cuts[k][1] for _, _, k in order[: order.index(chunk)])

    def turns(self, owner, j):
        h, u, i = j // self.half, j % self.half // self.m, j % self.m
        me = [(self.unit(owner, h, self.n - 1) - h * self.half) // self.m for h in range(2)]
        t = self.n - 1 - jnp.bitwise_xor(u, jnp.where(h == 0, me[0], me[1]))
        found = []
        for order in (self.made, self.pulled):
            place = jnp.zeros_like(j)
            for chunk in order:
                start, size = self.cuts[chunk[2]]
                at = (chunk[1] * 2 + chunk[0]) * self.m + start
                which = (t * 2 + h) * self.m + i - at
                place = jnp.where((which >= 0) & (which < size), self.turn(order, chunk) + which, place)
            found.append(place)
        return found

    def phase(self, t):
        p = 0
        while t >= self.n - (self.n >> (p + 1)):
            p += 1
        return p


def fill_tables(plan, per_dev, kernels, owner, strip, strips, inter, index, psf_index, table, tell):
    e, width = plan.exposures, inter.shape[0]
    where = inter[...]
    match = where // (strips * per_dev) == owner
    place = (where // per_dev % strips - strip + 1) * per_dev + where % per_dev

    def pick(values):
        return jnp.sum(jnp.where(match, values, 0), axis=0, keepdims=True)

    live = pick(jnp.ones_like(where)) > 0
    slot = jnp.where(live, jnp.clip(pick(place), 0, 3 * per_dev - 1), -1)
    kernel_of = index[...]
    table[pl.ds(ROW, 1), :] = jnp.where(live, pick(kernel_of[:width]), kernels)
    table[pl.ds(COL, 1), :] = pick(kernel_of[width:])
    table[pl.ds(PSF, 1), :] = psf_index[...]

    down = lax.broadcasted_iota(jnp.int32, (e, e), 0)
    along = lax.broadcasted_iota(jnp.int32, (e, e), 1)
    first_along, last_along = plan.turns(owner, along[:1])

    def upright(line):
        return jnp.sum(jnp.where(down == along, line, 0), axis=1, keepdims=True)

    def flat(column):
        return jnp.sum(jnp.where(down == along, column, 0), axis=0, keepdims=True)

    slot_down, last_down = upright(slot), upright(last_along)
    before = (slot_down == slot) & (last_down < last_along)
    table[pl.ds(PREV, 1), :] = jnp.max(jnp.where(before, last_down + 1, 0), axis=0, keepdims=True)

    ready = jnp.where(live, slot, per_dev)
    for side, last_row in ((0, LAST_LOW), (1, LAST_OWN), (2, LAST_HIGH)):
        near = slot - side * per_dev
        near = jnp.where((near >= 0) & (near < per_dev) & live, near, -1)
        hit = near == down
        last = jnp.max(jnp.where(hit, last_along + 1, 0), axis=1, keepdims=True)
        if side == 1:
            table[pl.ds(last_row, 1), :] = flat(last)
            continue
        line = down[:, :1]
        first = jnp.min(jnp.where(hit, first_along, e + down), axis=1, keepdims=True)
        rank = jnp.sum(jnp.where(flat(first) < first, 1, 0), axis=1, keepdims=True)
        give = jnp.sum(jnp.where(rank == along, down, 0), axis=0, keepdims=True)
        arrival = jnp.sum(jnp.where(hit, rank, 0), axis=0, keepdims=True)
        ready = jnp.where(near >= 0, side * per_dev + arrival, ready)
        order = jnp.where(line < per_dev, last, e + 1) * e + line
        order_along = flat(order)
        done = jnp.sum(jnp.where(order_along < order, 1, 0), axis=1, keepdims=True)
        table[pl.ds(last_row, 1), :] = jnp.sum(jnp.where(done == along, last, 0), axis=0, keepdims=True)
        up = side // 2
        tell[up, pl.ds(GIVE, 1), :] = jnp.clip(give, 0, per_dev - 1)
        tell[up, pl.ds(RANK, 1), :] = jnp.clip(flat(done), 0, per_dev - 1)
    table[pl.ds(READY, 1), :] = ready


def gradient_kernel(
    plan, per_dev, inter, index, psf_index, scene, observed, weights, bank_h, psf_h, out,
    inter_v, index_v, psf_v, table_v, tell_v, table, tell, told, ready, stage, came, bank, bank_t, psf, psf_t, obs, ivar, terms, got,
    adj, run, leave, back, load_sem, tell_send, tell_recv, z_send, z_recv, rs_send, rs_recv, ag_send,
    ag_recv, back_send, back_recv,
):
    n, m = plan.n, plan.m
    e = plan.exposures
    kernels = bank_h.shape[0]
    owner = lax.axis_index("scene")
    strip = lax.axis_index("expo")
    strips = lax.axis_size("expo")
    ahead, behind = cut(per_dev, EDGE, CHUNK), cut(per_dev, CHUNK, EDGE)
    has = {0: strip > 0, 1: strip < strips - 1}

    barrier = pltpu.get_barrier_semaphore()
    for p in range(plan.bits):
        pl.semaphore_signal(
            barrier, inc=1, device_id={"scene": plan.partner(owner, 0, p)}, device_id_type=MESH
        )
    for up in range(2):

        @pl.when(has[up])
        def _(up=up):
            pl.semaphore_signal(
                barrier, inc=1, device_id={"expo": strip + 2 * up - 1}, device_id_type=MESH
            )

    given = [
        pltpu.make_async_copy(source, target, load_sem.at[9 + i])
        for i, (source, target) in enumerate(((inter, inter_v), (index, index_v), (psf_index, psf_v)))
    ]
    for load in given:
        load.start()
    loads = [
        pltpu.make_async_copy(scene, ready.at[pl.ds(per_dev, per_dev)], load_sem.at[0]),
        pltpu.make_async_copy(bank_h, bank.at[pl.ds(0, kernels)], load_sem.at[1]),
        pltpu.make_async_copy(psf_h, psf, load_sem.at[2]),
    ]
    for h in range(2):
        home = plan.unit(owner, h, n - 1)
        for source, target in ((observed, obs), (weights, ivar)):
            loads.append(
                pltpu.make_async_copy(
                    source.at[pl.ds(home, m)], target.at[pl.ds(h * m, m)], load_sem.at[len(loads)]
                )
            )
    for load in loads:
        load.start()

    for load in given:
        load.wait()
    fill_tables(
        plan, per_dev, kernels, owner, strip, strips, inter_v, index_v, psf_v, table_v, tell_v
    )
    own_table = pltpu.make_async_copy(table_v, table, load_sem.at[7])
    own_tell = pltpu.make_async_copy(tell_v, tell, load_sem.at[8])
    own_tell.start()
    own_table.start()
    own_tell.wait()
    pl.semaphore_wait(
        barrier, plan.bits + jnp.where(has[0], 1, 0) + jnp.where(has[1], 1, 0)
    )

    def tell_copy(up):
        return pltpu.make_async_remote_copy(
            src_ref=tell.at[up],
            dst_ref=told.at[1 - up],
            send_sem=tell_send.at[up],
            recv_sem=tell_recv.at[1 - up],
            device_id={"expo": strip + 2 * up - 1},
            device_id_type=MESH,
        )

    for up in range(2):

        @pl.when(has[up])
        def _(up=up):
            tell_copy(up).start()

    bank[kernels] = jnp.zeros(bank.shape[1:], bank.dtype)
    bank_t[kernels] = jnp.zeros(bank.shape[1:], bank.dtype)
    run[0] = jnp.zeros(run.shape[1:], run.dtype)
    loads[0].wait()
    for up in range(2):

        @pl.when(jnp.logical_not(has[up]))
        def _(up=up):
            def wipe(i, carry):
                told[up, RANK, i] = 0
                back[up * per_dev + i] = jnp.zeros(back.shape[1:], back.dtype)
                return carry

            lax.fori_loop(0, per_dev, wipe, 0)

        @pl.when(has[up])
        def _(up=up):
            tell_copy(1 - up).wait_recv()

    def z_copy(up, q):
        start, size = ahead[q]
        return pltpu.make_async_remote_copy(
            src_ref=stage.at[pl.ds(up * per_dev + start, size)],
            dst_ref=came.at[pl.ds(up * per_dev + start, size)],
            send_sem=z_send.at[up * len(ahead) + q],
            recv_sem=z_recv.at[up * len(ahead) + q],
            device_id={"expo": strip + 2 * up - 1},
            device_id_type=MESH,
        )

    for q, (start, size) in enumerate(ahead):
        for up in range(2):

            @pl.when(has[up])
            def _(up=up, q=q, start=start, size=size):
                for i in range(start, start + size):
                    stage[up * per_dev + i] = ready[per_dev + told[up, GIVE, i]]
                z_copy(up, q).start()

    for load in loads[1:]:
        load.wait()

    turn_steps = [t for _, t, _ in plan.made].index(n - 1)

    def turn_some(step):
        for source, target, count in ((bank, bank_t, kernels), (psf, psf_t, psf.shape[0])):

            def turn(i, carry, source=source, target=target):
                target[i] = source[i].T
                return carry

            lax.fori_loop(step * count // turn_steps, (step + 1) * count // turn_steps, turn, 0)

    own_table.wait()
    taken = [0]

    def take(turns):
        while taken[0] < len(ahead) and ahead[taken[0]][0] < turns:
            q = taken[0]
            taken[0] += 1
            for up in range(2):

                @pl.when(has[1 - up])
                def _(up=up, q=q):
                    z_copy(up, q).wait_recv()
                    for i in range(ahead[q][0], sum(ahead[q])):
                        ready[(1 - up) * 2 * per_dev + i] = came[up * per_dev + i]

    def spot(h, t, k):
        return plan.base(h, t) + plan.cuts[k][0], plan.cuts[k][1]

    def slot(h, t, k):
        return (h * n + t) * plan.chunks + k

    def scatter_copy(h, t, k):
        return pltpu.make_async_remote_copy(
            src_ref=terms.at[pl.ds(*spot(h, t, k))],
            dst_ref=got.at[pl.ds(*spot(h, t, k))],
            send_sem=rs_send.at[slot(h, t, k)],
            recv_sem=rs_recv.at[slot(h, t, k)],
            device_id={"scene": plan.partner(owner, h, plan.phase(t))},
            device_id_type=MESH,
        )

    def gather_copy(h, t, p, k):
        target = t - (n >> (p + 1))
        return pltpu.make_async_remote_copy(
            src_ref=adj.at[pl.ds(*spot(h, t, k))],
            dst_ref=adj.at[pl.ds(*spot(h, target, k))],
            send_sem=ag_send.at[slot(h, target, k)],
            recv_sem=ag_recv.at[slot(h, target, k)],
            device_id={"scene": plan.partner(owner, h, p)},
            device_id_type=MESH,
        )

    def make_terms(h, t, k):
        where, size = spot(h, t, k)
        first = plan.unit(owner, h, t) + plan.cuts[k][0]
        inner = [
            dot(ready[table[READY, first + a]], bank[table[COL, first + a]], NT).astype(jnp.bfloat16)
            for a in range(size)
        ]
        term = [
            dot(bank[table[ROW, first + a]], x, NN).astype(jnp.bfloat16) for a, x in enumerate(inner)
        ]
        for a, x in enumerate(term):
            terms[where + a] = x

    def arrived(t):
        return [t - (n >> (q + 1)) for q in range(plan.bits) if t >= n - (n >> (q + 1))]

    def summed(h, t, k, i):
        total = terms[spot(h, t, k)[0] + i].astype(jnp.float32)
        for source in arrived(t):
            total = total + got[spot(h, source, k)[0] + i].astype(jnp.float32)
        return total.astype(jnp.bfloat16)

    def pass_on(h, t, k):
        where, size = spot(h, t, k)
        for i in range(size):
            terms[where + i] = summed(h, t, k, i)

    def psf_pass(h, k):
        where, size = spot(h, n - 1, k)
        start = plan.cuts[k][0]
        first = plan.unit(owner, h, n - 1) + start
        which = [table[PSF, first + a] for a in range(size)]
        half = [dot(summed(h, n - 1, k, a), psf[q], NT).astype(jnp.bfloat16) for a, q in enumerate(which)]
        model = [dot(psf[q], x, NN) for q, x in zip(which, half)]
        weighted = []
        for a, x in enumerate(model):
            here = h * m + start + a
            x = ivar[here].astype(jnp.float32) * (x - obs[here].astype(jnp.float32))
            weighted.append(x.astype(jnp.bfloat16))
        half = [dot(x, psf[q], NN).astype(jnp.bfloat16) for q, x in zip(which, weighted)]
        for a, (q, x) in enumerate(zip(which, half)):
            adj[where + a] = dot(psf_t[q], x, NN).astype(jnp.bfloat16)

    def back_copy(up, q):
        start, size = behind[q]
        return pltpu.make_async_remote_copy(
            src_ref=leave.at[pl.ds(up * per_dev + start, size)],
            dst_ref=back.at[pl.ds((1 - up) * per_dev + start, size)],
            send_sem=back_send.at[up * len(behind) + q],
            recv_sem=back_recv.at[(1 - up) * len(behind) + q],
            device_id={"expo": strip + 2 * up - 1},
            device_id_type=MESH,
        )

    def pull(h, t, k):
        where, size = spot(h, t, k)
        first = plan.unit(owner, h, t) + plan.cuts[k][0]
        turn = plan.turn(plan.pulled, [h, t, k])
        spread = [
            dot(adj[where + a], bank[table[COL, first + a]], NN).astype(jnp.bfloat16) for a in range(size)
        ]
        pulled = [dot(bank_t[table[ROW, first + a]], x, NN) for a, x in enumerate(spread)]
        for a, x in enumerate(pulled):
            run[1 + turn + a] = x + run[table[PREV, first + a]]

        for q, (start, count) in enumerate(behind):
            if turn < max(1, e - per_dev + start + count) <= turn + size:
                for up, last in ((0, LAST_LOW), (1, LAST_HIGH)):

                    @pl.when(has[up])
                    def _(up=up, last=last, q=q, start=start, count=count):
                        for a in range(start, start + count):
                            leave[up * per_dev + a] = run[table[last, a]].astype(leave.dtype)
                        back_copy(up, q).start()

    for number, (pulls, h, t, k) in enumerate(plan.steps):
        if pulls:
            if t < n - 1:
                last = plan.phase(t)
                gather_copy(h, t + (n >> (last + 1)), last, k).wait_recv()
                for p in reversed(range(last)):
                    gather_copy(h, t, p, k).start()
            pull(h, t, k)
            continue
        take(plan.turn(plan.made, [h, t, k]) + plan.cuts[k][1])
        make_terms(h, t, k)
        for source in arrived(t):
            scatter_copy(h, source, k).wait_recv()
        if t < n - 1:
            if t >= n // 2:
                pass_on(h, t, k)
            scatter_copy(h, t, k).start()
        else:
            psf_pass(h, k)
            for p in reversed(range(plan.bits)):
                gather_copy(h, n - 1, p, k).start()
        if number < turn_steps:
            turn_some(number)

    for up in range(2):

        @pl.when(has[up])
        def _(up=up):
            tell_copy(up).wait_send()
            for q in range(len(ahead)):
                z_copy(up, q).wait_send()

    for t in range(n - 1):
        for k in range(plan.chunks):
            for h in range(2):
                scatter_copy(h, t, k).wait_send()
                p = plan.phase(t)
                gather_copy(h, t + (n >> (p + 1)), p, k).wait_send()

    for up in range(2):

        @pl.when(has[up])
        def _(up=up):
            for q in range(len(behind)):
                back_copy(1 - up, q).wait_recv()

    def own(b, carry):
        low = back[told[0, RANK, b]].astype(jnp.float32)
        high = back[per_dev + told[1, RANK, b]].astype(jnp.float32)
        out[b] = run[table[LAST_OWN, b]] + (low + high)
        return carry

    lax.fori_loop(0, per_dev, own, 0, unroll=4)

    for up in range(2):

        @pl.when(has[up])
        def _(up=up):
            for q in range(len(behind)):
                back_copy(up, q).wait_send()


def on_device(
    scene,
    observed,
    inverse_variance,
    intersection,
    resample_index,
    psf_index,
    resample_bank,
    psf_bank,
):
    per_dev, side = scene.shape[0], scene.shape[1:]
    e = intersection.shape[0]
    plan = Plan(lax.axis_size("scene"), e)
    slots = 2 * plan.n * plan.chunks
    pieces = len(cut(per_dev, EDGE, EDGE)) + 1
    kernels, psfs = resample_bank.shape[0], psf_bank.shape[0]
    dtype = scene.dtype
    hbm = pl.BlockSpec(memory_space=pl.ANY)
    dma = pltpu.SemaphoreType.DMA
    blocks = lambda count, kind=dtype: pltpu.VMEM((count, *side), kind)
    return pl.pallas_call(
        functools.partial(gradient_kernel, plan, per_dev),
        out_shape=pltpu.VMEM((per_dev, *side), jnp.float32),
        in_specs=[hbm] * 8,
        out_specs=pl.BlockSpec(memory_space=pltpu.VMEM),
        scratch_shapes=[
            pltpu.VMEM((intersection.shape[1], e), jnp.int32),
            pltpu.VMEM((resample_index.shape[1], e), jnp.int32),
            pltpu.VMEM((1, e), jnp.int32),
            pltpu.VMEM((8, e), jnp.int32),
            pltpu.VMEM((2, 2, e), jnp.int32),
            pltpu.SMEM((8, e), jnp.int32),
            pltpu.SMEM((2, 2, e), jnp.int32),
            pltpu.SMEM((2, 2, e), jnp.int32),
            blocks(3 * per_dev),
            blocks(2 * per_dev),
            blocks(2 * per_dev),
            blocks(kernels + 1),
            blocks(kernels + 1),
            blocks(psfs),
            blocks(psfs),
            blocks(2 * plan.m),
            blocks(2 * plan.m),
            blocks(e),
            blocks(e),
            blocks(e),
            blocks(e + 1, jnp.float32),
            blocks(2 * per_dev),
            blocks(2 * per_dev),
            dma((12,)),
            dma((2,)),
            dma((2,)),
            dma((2 * pieces,)),
            dma((2 * pieces,)),
            dma((slots,)),
            dma((slots,)),
            dma((slots,)),
            dma((slots,)),
            dma((2 * pieces,)),
            dma((2 * pieces,)),
        ],
        compiler_params=pltpu.CompilerParams(
            collective_id=0, has_side_effects=True, vmem_limit_bytes=VMEM_LIMIT
        ),
        name="gradient",
    )(
        intersection.T, resample_index.T, psf_index.reshape(1, e), scene, observed, inverse_variance,
        resample_bank, psf_bank,
    )


def solution(mesh):
    return jax.shard_map(
        on_device,
        mesh=mesh,
        in_specs=(
            P(("scene", "expo"), None, None),
            P("expo", None, None),
            P("expo", None, None),
            P("expo", None),
            P("expo", None),
            P("expo"),
            P(),
            P(),
        ),
        out_specs=P(("scene", "expo"), None, None),
        check_vma=False,
    )
```
